256 devices in a mesh: dp: 4 (over y), ctx: 64 (over x, z, core).
Axes of the slice: x: 4, y: 4, z: 8, core: 2. Of those that a mesh axis runs over, the one named last changes fastest.
Arguments:
- query_rows: bfloat16 [262144, 1024], P(('dp', 'ctx')), parts along dimension 0, may hold values from -6 to 6
- key_rows: bfloat16 [262144, 1024], P(('dp', 'ctx')), parts along dimension 0, may hold values from -6 to 6
- value_rows: bfloat16 [262144, 1024], P(('dp', 'ctx')), parts along dimension 0, may hold values from -6 to 6
- lengths: int32 [512], P('dp'), parts along dimension 0, may hold values from 1 to 40960, as said below
- conv_weight: float32 [3, 4, 1024], replicated, may hold values from -3 to 3
- out_gain: float32 [1024], replicated, may hold values from 0.1 to 1.9
Outputs:
- mixed: bfloat16 [262144, 1024], P(('dp', 'ctx')), parts along dimension 0
The draws below stay inside these ranges and needn't reach their ends.
There are 4 independent parts, one for each index of `dp`. The reference program is written for one: setup_inputs(seed, part) draws one part's arguments, and reference() takes and returns one part's arrays. A program takes and returns all parts, laid end to end along the dimension named above; an argument that names none is the same for every part. Nothing has to cross between parts.
Inputs may be any that keep to these rules, and one draw needn't show every extreme that they name: The lengths of one part sum to 65536; the last document has exactly 40960 tokens.
All inputs are finite; a program needn't handle non-finite values.
Results may differ from the reference program's by a relative error of at most 0.0065.
Values may be sent and summed in bfloat16 or wider, within the bound.
No kernel may reach another device: no remote copies, remote signals or barrier semaphores. Data moves between devices by JAX's collectives and lax.ppermute only.
A program may use at most 128 MiB of HBM per device.

```python
import jax
import jax.numpy as jnp
from jax import lax

HEADS = 8
HEAD = 128
TOK_DEV = 1024
TOKENS = 65536
MOST = 40960
NDOC = 128
N_CTX = 64


def draw_lengths(key, part):
    rest = TOKENS - MOST
    half = MOST // 2
    points = jnp.arange(1, rest, dtype=jnp.int32)
    ranks = jax.random.permutation(jax.random.fold_in(key, 11), rest - 1).astype(jnp.int32)
    forced = points % half == 0
    ranks = jnp.where(forced, -1 - points, ranks)
    order = jnp.argsort(ranks, stable=True)
    chosen = jnp.sort(points[order[:NDOC - 2]])
    bounds = jnp.concatenate([jnp.zeros((1,), jnp.int32), chosen, jnp.full((1,), rest, jnp.int32)])
    pieces = bounds[1:] - bounds[:-1]
    return jnp.concatenate([pieces, jnp.full((1,), MOST, jnp.int32)]).astype(jnp.int32)


def levels(key, extent, split, low, top_value):
    def one(dim, shards_of):
        steps = jax.random.uniform(jax.random.fold_in(jax.random.fold_in(key, 6), dim), (shards_of,), jnp.float32, low / len(split), top_value / len(split))
        return jnp.repeat(jnp.exp(steps), extent[dim] // shards_of).reshape((-1,) + (1,) * (len(extent) - dim - 1))

    level = one(*split[0])
    for cut in split[1:]:
        level = level * one(*cut)
    return level


def gaussian(own_key, extent, deviation, limit, shards=(), kind=jnp.bfloat16):
    gain = levels(own_key, extent, shards, -0.22, 0.18) if shards else 1.0
    array = jax.random.normal(own_key, extent, jnp.float32) * deviation * gain
    return jnp.minimum(jnp.maximum(array, -limit), limit).astype(kind)


def setup_inputs(seed: int = 0, part: int = 0) -> dict:
    splits = jax.random.split(jax.random.key(seed), 7)
    own_keys = jax.random.split(jax.random.fold_in(splits[6], part), 7)
    query_rows = gaussian(own_keys[0], (TOKENS, HEADS * HEAD), 1.0, 6.0, ((0, 64),))
    key_rows = gaussian(own_keys[1], (TOKENS, HEADS * HEAD), 1.0, 6.0, ((0, 64),))
    value_rows = gaussian(own_keys[2], (TOKENS, HEADS * HEAD), 1.0, 6.0, ((0, 64),))
    lengths = draw_lengths(jax.random.fold_in(jax.random.fold_in(splits[6], part), 71), part)
    conv_weight = gaussian(splits[4], (3, 4, HEADS * HEAD), 0.5, 3.0, (), jnp.float32)
    out_gain = jnp.clip(1.0 + 0.18 * jax.random.normal(splits[5], (HEADS * HEAD,), jnp.float32), 0.1, 1.9)
    return {"query_rows": query_rows, "key_rows": key_rows, "value_rows": value_rows, "lengths": lengths, "conv_weight": conv_weight, "out_gain": out_gain}


def doc_lookup(starts, positions):
    return lax.optimization_barrier(jnp.sum((starts[None, :] <= positions[:, None]).astype(jnp.int32), axis=1)) - 1

def features(extended, doc_ext, conv_weight, row_count):
    made = []
    for which in range(3):
        summed = jnp.zeros((row_count, extended[which].shape[1]), jnp.float32)
        for delay in range(4):
            same_doc = (doc_ext[3 - delay:3 - delay + row_count] == doc_ext[3:]).astype(jnp.float32)
            shifted = extended[which][3 - delay:3 - delay + row_count].astype(jnp.float32)
            summed = summed + conv_weight[which, delay][None, :] * shifted * same_doc[:, None]
        made.append(summed)
    return (jax.nn.silu(made[0]).astype(jnp.bfloat16), jax.nn.silu(made[1]).astype(jnp.bfloat16), made[2].astype(jnp.bfloat16))

def mix_block(query_part, key_part, value_part, state_bf, use_in, doc_ids, out_gain):
    row_count = query_part.shape[0]
    block = min(512, row_count)
    pieces = []
    for block_id in range(row_count // block):
        opening = block_id * block
        closing = opening + block
        scores = jnp.einsum('qhd,khd->hqk', query_part[opening:closing].astype(jnp.float32), key_part[:closing].astype(jnp.float32))
        row_ids = jnp.arange(opening, closing)
        col_ids = jnp.arange(closing)
        allowed = (col_ids[None, :] <= row_ids[:, None]) & (doc_ids[:closing][None, :] == doc_ids[opening:closing][:, None])
        weights = jnp.where(allowed[None], scores, 0.0).astype(jnp.bfloat16)
        within = jnp.einsum('hqk,khe->qhe', weights.astype(jnp.float32), value_part[:closing].astype(jnp.float32))
        carried = jnp.einsum('qhd,hde->qhe', query_part[opening:closing].astype(jnp.float32), state_bf.astype(jnp.float32))
        pieces.append(within + carried * use_in[opening:closing, None, None])
    mixture = jnp.concatenate(pieces, axis=0)
    inverse_rms = lax.rsqrt(lax.optimization_barrier(jnp.mean(mixture * mixture, axis=-1, keepdims=True)) + 1e-06)
    normed = (mixture * inverse_rms).reshape(row_count, -1)
    return (normed * out_gain[None, :]).astype(jnp.bfloat16)

def reference(query_rows, key_rows, value_rows, lengths, conv_weight, out_gain):
    channels = query_rows.shape[1]
    starts = jnp.cumsum(lengths) - lengths
    padded = [jnp.pad(arr, ((3, 0), (0, 0))) for arr in (query_rows, key_rows, value_rows)]

    def advance(carried, device):
        offset = (device * TOK_DEV).astype(jnp.int32)
        positions = offset - 3 + jnp.arange(TOK_DEV + 3, dtype=jnp.int32)
        doc_ext = doc_lookup(starts, positions)
        extended = [lax.dynamic_slice_in_dim(arr, offset, TOK_DEV + 3, 0) for arr in padded]
        phi_q, phi_k, val = features(extended, doc_ext, conv_weight, TOK_DEV)
        doc_ids = doc_ext[3:]
        phi_q = phi_q.reshape(TOK_DEV, HEADS, HEAD)
        phi_k = phi_k.reshape(TOK_DEV, HEADS, HEAD)
        val = val.reshape(TOK_DEV, HEADS, HEAD)
        opens_here = jnp.any(starts == offset)
        use_in = ((doc_ids == doc_ids[0]) & jnp.logical_not(opens_here)).astype(jnp.float32)
        output = mix_block(phi_q, phi_k, val, carried.astype(jnp.bfloat16), use_in, doc_ids, out_gain)
        tail_mask = (doc_ids == doc_ids[-1]).astype(jnp.float32)
        tail_state = jnp.einsum('thd,the->hde', phi_k.astype(jnp.float32) * tail_mask[:, None, None], val.astype(jnp.float32))
        restart = jnp.any((starts >= offset) & (starts < offset + TOK_DEV))
        return (jnp.where(restart, tail_state, carried + tail_state), output)
    initial = jnp.zeros((HEADS, HEAD, HEAD), jnp.float32)
    _, outputs = lax.scan(advance, initial, jnp.arange(N_CTX, dtype=jnp.int32))
    return outputs.reshape(TOKENS, channels)
```

```python
import jax
import jax.numpy as jnp
from jax import lax
from jax.experimental import pallas as pl
from jax.experimental.pallas import tpu as pltpu
from jax.sharding import Mesh
from jax.sharding import PartitionSpec as P

HEAD = 128
CHUNK = 256
CTX = ("x", "z", "c")
DP_CTX = ("dp", "x", "z", "c")
F32 = jnp.float32
BF16 = jnp.bfloat16


def docs_at(first, count, starts_row):
    pos = (lax.broadcasted_iota(jnp.int32, (count, HEAD), 0) + first).astype(F32)
    below = jnp.where(starts_row <= pos, 1.0, 0.0).astype(BF16)
    ones = jnp.ones((HEAD, HEAD), BF16)
    return jnp.dot(below, ones, preferred_element_type=F32), below


def fill_masks(first, starts_ref, doc_s, m_s):
    rows = m_s.shape[1]
    doc, below = docs_at(first - 8, rows + 8, starts_ref[...])
    doc_s[...] = doc
    for j in (1, 2, 3):
        m_s[j - 1] = jnp.where(doc_s[8 - j : 8 - j + rows] == doc_s[8:], 1.0, 0.0)
    return below


def conv(ext, weight, m_s, r0, size):
    acc = weight[0:1] * ext[8 + r0 : 8 + r0 + size]
    for j in (1, 2, 3):
        acc += weight[j : j + 1] * (ext[8 + r0 - j : 8 + r0 - j + size] * m_s[j - 1, r0 : r0 + size])
    return acc


def silu(u):
    half = 0.5 * u
    return half * jnp.tanh(half) + half


def kv_kernel(off_ref, starts_ref, k_ref, v_ref, kr_ref, vr_ref, kw_ref, vw_ref, pk_ref, val_ref, st_ref, tail_ref, doc_s, m_s, ext_k, ext_v):
    rows = k_ref.shape[0]

    @pl.when(pl.program_id(0) == 0)
    def _():
        fill_masks(off_ref[0], starts_ref, doc_s, m_s)

    ext_k[0:8] = kr_ref[...].astype(F32)
    ext_v[0:8] = vr_ref[...].astype(F32)
    ext_k[8:] = k_ref[...].astype(F32)
    ext_v[8:] = v_ref[...].astype(F32)
    state = jnp.zeros((HEAD, HEAD), F32)
    for i in range(rows // CHUNK):
        r0 = i * CHUNK
        key = silu(conv(ext_k, kw_ref[...], m_s, r0, CHUNK)).astype(BF16)
        val = conv(ext_v, vw_ref[...], m_s, r0, CHUNK).astype(BF16)
        pk_ref[0, r0 : r0 + CHUNK] = key
        val_ref[0, r0 : r0 + CHUNK] = val
        last = doc_s[8 + r0 + CHUNK - 1 : 8 + r0 + CHUNK]
        live = jnp.where(doc_s[8 + r0 : 8 + r0 + CHUNK] == last, 1.0, 0.0).astype(BF16)
        tail = lax.dot_general(key * live, val, (((0,), (0,)), ((), ())), preferred_element_type=F32)
        keep = jnp.where(doc_s[8 + r0 - 1 : 8 + r0] == last, 1.0, 0.0)
        state = state * keep + tail
        if i < rows // CHUNK - 1:
            st_ref[0, i] = state
    tail_ref[0] = state.astype(BF16)


def attend_kernel(off_ref, starts_ref, q_ref, qr_ref, qw_ref, pk_ref, val_ref, pq_ref, mix_ref, doc_s, m_s, ext, allow_s):
    rows = q_ref.shape[0]

    @pl.when(pl.program_id(0) == 0)
    def _():
        below = fill_masks(off_ref[0], starts_ref, doc_s, m_s)
        across = lax.dot_general(
            jnp.ones((8, HEAD), BF16), below[8:], (((1,), (1,)), ((), ())), preferred_element_type=F32
        )
        row = lax.broadcasted_iota(jnp.int32, (CHUNK, CHUNK), 0)
        col = lax.broadcasted_iota(jnp.int32, (CHUNK, CHUNK), 1)
        for i in range(rows // CHUNK):
            r0 = i * CHUNK
            mine = jnp.concatenate([doc_s[8 + r0 : 8 + r0 + CHUNK]] * 2, axis=1)
            same = (mine == across[0:1, r0 : r0 + CHUNK]) & (col <= row)
            allow_s[i] = jnp.where(same, 1.0, 0.0).astype(BF16)

    ext[0:8] = qr_ref[...].astype(F32)
    ext[8:] = q_ref[...].astype(F32)
    for i in range(rows // CHUNK):
        r0 = i * CHUNK
        query = silu(conv(ext, qw_ref[...], m_s, r0, CHUNK)).astype(BF16)
        pq_ref[0, r0 : r0 + CHUNK] = query
        scores = lax.dot_general(
            query, pk_ref[0, r0 : r0 + CHUNK], (((1,), (1,)), ((), ())), preferred_element_type=F32
        )
        weights = scores.astype(BF16) * allow_s[i]
        mix_ref[0, r0 : r0 + CHUNK] = jnp.dot(weights, val_ref[0, r0 : r0 + CHUNK], preferred_element_type=F32)


def finish_kernel(off_ref, starts_ref, mix_ref, pq_ref, st_ref, own_ref, far_ref, gain_ref, out_ref, doc_s):
    rows = pq_ref.shape[1]
    step = pl.program_id(0)

    @pl.when(step == 0)
    def _():
        doc, _ = docs_at(off_ref[0] - 8, rows + 8, starts_ref[...])
        doc_s[...] = doc

    carried = jnp.where(step < pl.num_programs(0) // 2, own_ref[0], far_ref[0]).astype(F32)
    before = doc_s[7:8]
    for i in range(rows // CHUNK):
        r0 = i * CHUNK
        prior = doc_s[8 + r0 - 1 : 8 + r0]
        if i == 0:
            state = carried
        else:
            state = st_ref[0, i - 1] + carried * jnp.where(prior == before, 1.0, 0.0)
        use = jnp.where(doc_s[8 + r0 : 8 + r0 + CHUNK] == prior, 1.0, 0.0)
        held = jnp.dot(pq_ref[0, r0 : r0 + CHUNK], state.astype(BF16), preferred_element_type=F32)
        mixture = mix_ref[0, r0 : r0 + CHUNK] + held * use
        scale = lax.rsqrt(jnp.mean(mixture * mixture, axis=-1, keepdims=True) + 1e-06)
        out_ref[r0 : r0 + CHUNK] = (mixture * scale * gain_ref[...]).astype(BF16)


def per_device(query_rows, key_rows, value_rows, lengths, conv_weight, out_gain):
    rows, channels = query_rows.shape
    heads = channels // HEAD
    half = heads // 2
    x_here, z_here, core = lax.axis_index("x"), lax.axis_index("z"), lax.axis_index("c")
    z_count = lax.axis_size("z")
    x_count = lax.axis_size("x")
    ctx_count = x_count * z_count * 2
    here = lax.axis_index(CTX)
    offset = (here * rows).astype(jnp.int32)

    rims = jnp.stack([query_rows[rows - 8 :], key_rows[rows - 8 :], value_rows[rows - 8 :]])
    rims = lax.ppermute(rims, CTX, [(i, i + 1) for i in range(ctx_count - 1)])

    earlier = jnp.arange(lengths.shape[0])
    starts = jnp.sum(jnp.where(earlier[:, None] < earlier[None, :], lengths[:, None], 0), axis=0)
    row_first = x_here * z_count * 2 * rows
    chip_last = row_first + jnp.arange(z_count + 1) * 2 * rows - 1
    here_last = jnp.stack([offset - core * rows - 1, offset - core * rows + rows - 1, offset - core * rows + 2 * rows - 1])
    marks = jnp.concatenate([chip_last, here_last])
    doc_marks = jnp.sum((starts[None, :] <= marks[:, None]).astype(jnp.int32), axis=1)
    same = (doc_marks[1:] == doc_marks[:-1]).astype(F32)
    keep_chip = same[:z_count]
    keep_first, keep_second = same[z_count + 1], same[z_count + 2]

    offsets = offset.reshape(1)
    starts_row = starts.astype(F32).reshape(1, -1)
    smem = pl.BlockSpec(memory_space=pltpu.SMEM)
    whole = lambda shape: pl.BlockSpec(shape, lambda h: (0,) * len(shape))
    column = pl.BlockSpec((rows, HEAD), lambda h: (0, h))
    taps = lambda w: pl.BlockSpec((None, 4, HEAD), lambda h: (w, 0, h))
    rim = lambda w: pl.BlockSpec((None, 8, HEAD), lambda h: (w, 0, h))
    by_head = pl.BlockSpec((1, rows, HEAD), lambda h: (h, 0, 0))
    chunks = rows // CHUNK
    head_rows = (heads, rows, HEAD)
    arbitrary = pltpu.CompilerParams(dimension_semantics=("arbitrary",))

    phi_k, val, inner, tail = pl.pallas_call(
        kv_kernel,
        grid=(heads,),
        in_specs=[smem, whole((1, HEAD)), column, column, rim(1), rim(2), taps(1), taps(2)],
        out_specs=[
            by_head,
            by_head,
            pl.BlockSpec((1, chunks - 1, HEAD, HEAD), lambda h: (h, 0, 0, 0)),
            pl.BlockSpec((1, HEAD, HEAD), lambda h: (h, 0, 0)),
        ],
        out_shape=[
            jax.ShapeDtypeStruct(head_rows, BF16),
            jax.ShapeDtypeStruct(head_rows, BF16),
            jax.ShapeDtypeStruct((heads, chunks - 1, HEAD, HEAD), F32),
            jax.ShapeDtypeStruct((heads, HEAD, HEAD), BF16),
        ],
        scratch_shapes=[
            pltpu.VMEM((rows + 8, HEAD), F32),
            pltpu.VMEM((3, rows, HEAD), F32),
            pltpu.VMEM((rows + 8, HEAD), F32),
            pltpu.VMEM((rows + 8, HEAD), F32),
        ],
        compiler_params=arbitrary,
        name="kv",
    )(offsets, starts_row, key_rows, value_rows, rims, rims, conv_weight, conv_weight)

    phi_q, mix = pl.pallas_call(
        attend_kernel,
        grid=(heads,),
        in_specs=[smem, whole((1, HEAD)), column, rim(0), taps(0), by_head, by_head],
        out_specs=[by_head, by_head],
        out_shape=[jax.ShapeDtypeStruct(head_rows, BF16), jax.ShapeDtypeStruct(head_rows, F32)],
        scratch_shapes=[
            pltpu.VMEM((rows + 8, HEAD), F32),
            pltpu.VMEM((3, rows, HEAD), F32),
            pltpu.VMEM((rows + 8, HEAD), F32),
            pltpu.VMEM((chunks, CHUNK, CHUNK), BF16),
        ],
        compiler_params=arbitrary,
        name="attend",
    )(offsets, starts_row, query_rows, rims, conv_weight, phi_k, val)

    first_core = core == 0
    own = lax.dynamic_slice_in_dim(tail, core * half, half, 0)
    other = lax.dynamic_slice_in_dim(tail, (1 - core) * half, half, 0)
    swap = [(0, 1), (1, 0)]
    got = lax.ppermute(other, "c", swap)
    tail_first = jnp.where(first_core, own, got).astype(F32)
    tail_second = jnp.where(first_core, got, own).astype(F32)
    chip_tail = (tail_first * keep_second + tail_second).astype(BF16)
    spread = lax.all_to_all(chip_tail.reshape(z_count, -1, HEAD), "z", 0, 0, tiled=True)
    spread = spread.astype(F32)
    row_total = jnp.zeros(spread.shape[1:], F32)
    for z in range(z_count):
        row_total = row_total * keep_chip[z] + spread[z]
    near = lax.ppermute(row_total, "x", [(i, i + 1) for i in range(x_count - 1)])
    far = lax.ppermute(row_total, "x", [(1, 3)])
    running = near + far
    entering = []
    for z in range(z_count):
        entering.append(running.astype(BF16))
        running = running * keep_chip[z] + spread[z]
    entered = lax.all_to_all(jnp.stack(entering), "z", 0, 0, tiled=True)
    carried_first = entered.reshape(half, HEAD, HEAD)
    carried_second = (carried_first.astype(F32) * keep_first + tail_first).astype(BF16)
    carried_own = jnp.where(first_core, carried_first, carried_second)
    carried_other = jnp.where(first_core, carried_second, carried_first)
    carried_far = lax.ppermute(carried_other, "c", swap)

    place = jnp.stack([offset, core.astype(jnp.int32)])
    head_of = lambda h, s: jnp.where(h < half, h + s[1] * half, h - s[1] * half)
    return pl.pallas_call(
        finish_kernel,
        grid_spec=pltpu.PrefetchScalarGridSpec(
            num_scalar_prefetch=1,
            grid=(heads,),
            in_specs=[
                pl.BlockSpec((1, HEAD), lambda h, s: (0, 0)),
                pl.BlockSpec((1, rows, HEAD), lambda h, s: (head_of(h, s), 0, 0)),
                pl.BlockSpec((1, rows, HEAD), lambda h, s: (head_of(h, s), 0, 0)),
                pl.BlockSpec((1, chunks - 1, HEAD, HEAD), lambda h, s: (head_of(h, s), 0, 0, 0)),
                pl.BlockSpec((1, HEAD, HEAD), lambda h, s: (jnp.minimum(h, half - 1), 0, 0)),
                pl.BlockSpec((1, HEAD, HEAD), lambda h, s: (jnp.maximum(h - half, 0), 0, 0)),
                pl.BlockSpec((1, HEAD), lambda h, s: (0, head_of(h, s))),
            ],
            out_specs=pl.BlockSpec((rows, HEAD), lambda h, s: (0, head_of(h, s))),
            scratch_shapes=[pltpu.VMEM((rows + 8, HEAD), F32)],
        ),
        out_shape=jax.ShapeDtypeStruct((rows, channels), BF16),
        compiler_params=arbitrary,
        name="finish",
    )(place, starts_row, mix, phi_q, inner, carried_own, carried_far, out_gain.reshape(1, -1))


def solution(mesh):
    finer = Mesh(mesh.devices.reshape(mesh.shape["dp"], 4, 8, 2), DP_CTX)
    return jax.shard_map(
        per_device,
        mesh=finer,
        in_specs=(P(DP_CTX, None), P(DP_CTX, None), P(DP_CTX, None), P("dp"), P(), P()),
        out_specs=P(DP_CTX, None),
        check_vma=False,
    )
```

```python
import jax
import jax.numpy as jnp
from jax import lax
from jax.experimental import pallas as pl
from jax.experimental.pallas import tpu as pltpu
from jax.sharding import Mesh
from jax.sharding import PartitionSpec as P

HEAD = 128
PAIR = 2 * HEAD
CHUNK = 256
GROUP = 16
CTX = ("x", "z", "c")
DP_CTX = ("dp", "x", "z", "c")
F32 = jnp.float32
BF16 = jnp.bfloat16


def one_if(flag):
    return jnp.where(flag, 1.0, 0.0)


def starts_of(lengths):
    rows = jnp.broadcast_to(lengths, (8, HEAD))
    before = one_if(
        lax.broadcasted_iota(jnp.int32, (HEAD, HEAD), 0) < lax.broadcasted_iota(jnp.int32, (HEAD, HEAD), 1)
    ).astype(BF16)
    high = jnp.dot((rows >> 8).astype(F32).astype(BF16), before, preferred_element_type=F32)
    low = jnp.dot((rows & 255).astype(F32).astype(BF16), before, preferred_element_type=F32)
    return high * 256.0 + low


def docs_of(positions, starts):
    below = one_if(starts[0:1] <= positions.astype(F32)).astype(BF16)
    return jnp.dot(below, jnp.ones((HEAD, HEAD), BF16), preferred_element_type=F32), below


def wide(rows):
    return jnp.concatenate([rows, rows], axis=1)


def fill_doc(first, starts, doc_s, m_s):
    count = m_s.shape[1]
    iota = lax.broadcasted_iota(jnp.int32, (count + 8, HEAD), 0)
    doc, below = docs_of(iota + (first - 8), starts)
    doc_s[...] = doc
    for j in (1, 2, 3):
        m_s[j - 1] = one_if(doc_s[8 - j : 8 - j + count] == doc_s[8:])
    return below


def conv(ext, taps, m_s, r0):
    acc = taps[0:1] * ext[8 + r0 : 8 + r0 + CHUNK]
    for j in (1, 2, 3):
        acc += taps[j : j + 1] * (ext[8 + r0 - j : 8 + r0 - j + CHUNK] * m_s[j - 1, r0 : r0 + CHUNK])
    return acc


def silu_of_half(half):
    return half * jnp.tanh(half) + half


def kv_chunk(ext_k, ext_v, kw, vw, doc, m_s, r0):
    key = silu_of_half(conv(ext_k, kw, m_s, r0)).astype(BF16)
    val = conv(ext_v, vw, m_s, r0).astype(BF16)
    live = one_if(doc[8 + r0 : 8 + r0 + CHUNK] == doc[8 + r0 + CHUNK - 1 : 8 + r0 + CHUNK]).astype(BF16)
    tail = lax.dot_general(key * live, val, (((0,), (0,)), ((), ())), preferred_element_type=F32)
    return key, val, tail


def late_kernel(
    here_ref, len_ref, k_ref, v_ref, kw_ref, vw_ref,
    pk_ref, val_ref, st_ref, gate_ref, doc_s, m_s, ext_k, ext_v,
    *, chips,
):
    rows = k_ref.shape[0]
    chunks = rows // CHUNK

    @pl.when(pl.program_id(0) == 0)
    def _():
        here = here_ref[0]
        core = here % 2
        offset = here * rows
        starts = starts_of(len_ref[...])
        fill_doc(offset, starts, doc_s, m_s)
        chip = offset - core * rows
        first = (here // (2 * chips)) * (2 * chips * rows)
        mark = lax.broadcasted_iota(jnp.int32, (16, HEAD), 0)
        ends, _ = docs_of(first + mark * (2 * rows) - 1, starts)
        mine, _ = docs_of(chip + mark * rows - 1, starts)
        inner, _ = docs_of(offset + mark * CHUNK - 1, starts)
        keep_first = one_if(mine[1:2] == mine[0:1])
        keep_second = one_if(mine[2:3] == mine[1:2])
        second = jnp.full((1, HEAD), core, jnp.int32) == 1
        gate_ref[0:chips] = one_if(ends[1 : chips + 1] == ends[0:chips])
        one, zero = jnp.ones((1, HEAD), F32), jnp.zeros((1, HEAD), F32)
        rest = [
            jnp.where(second, one, keep_second),
            jnp.where(second, keep_second, one),
            jnp.where(second, keep_first, one),
            jnp.where(second, one, zero),
            jnp.where(second, one, keep_first),
            jnp.where(second, zero, one),
        ]
        for n, row in enumerate(rest):
            gate_ref[chips + n : chips + n + 1] = row
        for i in range(1, chunks):
            gate_ref[chips + 7 + i : chips + 8 + i] = one_if(inner[i : i + 1] == inner[0:1])
        for i in range(2, chunks + 1):
            gate_ref[chips + 9 + i : chips + 10 + i] = one_if(inner[i : i + 1] == inner[1:2])

    for n in (0, 1):
        cols = slice(n * HEAD, (n + 1) * HEAD)
        ext_k[n, CHUNK - 8 :] = k_ref[CHUNK - GROUP :, cols].astype(F32)
        ext_v[n, CHUNK - 8 :] = v_ref[CHUNK - GROUP :, cols].astype(F32)
    states = [jnp.zeros((HEAD, HEAD), F32)] * 2
    for i in range(1, chunks):
        r0 = i * CHUNK
        same = one_if(doc_s[8 + r0 - 1 : 8 + r0] == doc_s[8 + r0 + CHUNK - 1 : 8 + r0 + CHUNK])
        for n in (0, 1):
            cols = slice(n * HEAD, (n + 1) * HEAD)
            key, val, tail = kv_chunk(
                ext_k.at[n], ext_v.at[n], 0.5 * kw_ref[:, cols], vw_ref[:, cols], doc_s, m_s, r0
            )
            pk_ref[n, r0 - CHUNK : r0] = key
            val_ref[n, r0 - CHUNK : r0] = val
            states[n] = states[n] * same + tail
            st_ref[n, i - 1] = states[n]


def first_kernel(
    here_ref, len_ref, gate_ref, k_ref, v_ref, kr_ref, vr_ref, kw_ref, vw_ref, late_ref, *rest, rows, chips,
):
    pk_ref, val_ref, st_ref, tail_ref, doc_s, m_s, ext_k, ext_v = rest[-8:]
    count = late_ref.shape[1] + 1

    @pl.when(pl.program_id(0) == 0)
    def _():
        fill_doc(here_ref[0] * rows, starts_of(len_ref[...]), doc_s, m_s)

    for n in (0, 1):
        cols = slice(n * HEAD, (n + 1) * HEAD)
        ext_k[n, 0:8] = kr_ref[:, cols].astype(F32)
        ext_v[n, 0:8] = vr_ref[:, cols].astype(F32)
        ext_k[n, 8:] = k_ref[:, cols].astype(F32)
        ext_v[n, 8:] = v_ref[:, cols].astype(F32)
    for n in (0, 1):
        cols = slice(n * HEAD, (n + 1) * HEAD)
        pk_ref[n], val_ref[n], tail = kv_chunk(
            ext_k.at[n], ext_v.at[n], 0.5 * kw_ref[:, cols], vw_ref[:, cols], doc_s, m_s, 0
        )
        st_ref[n, 0] = tail.astype(BF16)
        for i in range(1, count):
            state = late_ref[n, i - 1] + tail * gate_ref[chips + 10 + i : chips + 11 + i]
            if i < count - 1:
                st_ref[n, i] = state.astype(BF16)
        tail_ref[n] = state.astype(BF16)


def attend_kernel(
    here_ref, len_ref, q_ref, qr_ref, qw_ref, pkf_ref, pkl_ref, valf_ref, vall_ref, *rest,
):
    pq_ref, mix_ref, doc_s, m_s, ext, allow_s = rest[-6:]
    rows = q_ref.shape[0]
    chunks = rows // CHUNK

    @pl.when(pl.program_id(0) == 0)
    def _():
        below = fill_doc(here_ref[0] * rows, starts_of(len_ref[...]), doc_s, m_s)
        across = lax.dot_general(
            jnp.ones((8, HEAD), BF16), below[8:], (((1,), (1,)), ((), ())), preferred_element_type=F32
        )
        causal = lax.broadcasted_iota(jnp.int32, (CHUNK, CHUNK), 1) <= lax.broadcasted_iota(
            jnp.int32, (CHUNK, CHUNK), 0
        )
        for i in range(chunks):
            r0 = i * CHUNK
            same = wide(doc_s[8 + r0 : 8 + r0 + CHUNK]) == across[0:1, r0 : r0 + CHUNK]
            allow_s[i] = jnp.where(same & causal, 1.0, 0.0).astype(BF16)

    for n in (0, 1):
        cols = slice(n * HEAD, (n + 1) * HEAD)
        ext[n, 0:8] = qr_ref[:, cols].astype(F32)
        ext[n, 8:] = q_ref[:, cols].astype(F32)

    def make(i, n):
        cols = slice(n * HEAD, (n + 1) * HEAD)
        r0 = i * CHUNK
        query = silu_of_half(conv(ext.at[n], 0.5 * qw_ref[:, cols], m_s, r0)).astype(BF16)
        use = one_if(doc_s[8 + r0 : 8 + r0 + CHUNK] == doc_s[8 + r0 - 1 : 8 + r0]).astype(BF16)
        pq_ref[n, r0 : r0 + CHUNK] = query * use
        return query

    def mixed(i, n, query):
        r0 = i * CHUNK
        key = pkf_ref[n] if i == 0 else pkl_ref[n, r0 - CHUNK : r0]
        val = valf_ref[n] if i == 0 else vall_ref[n, r0 - CHUNK : r0]
        scores = lax.dot_general(query, key, (((1,), (1,)), ((), ())), preferred_element_type=F32)
        weights = scores.astype(BF16) * allow_s[i]
        mix_ref[n, r0 : r0 + CHUNK] = jnp.dot(weights, val, preferred_element_type=F32).astype(BF16)

    order = [(i, n) for i in range(chunks) for n in (0, 1)]
    ahead = None
    for at in order:
        query = make(*at)
        if ahead is not None:
            mixed(*ahead)
        ahead = at + (query,)
    mixed(*ahead)


def finish_kernel(here_ref, gate_ref, mix_ref, pq_ref, st_ref, carried_ref, gain_ref, *rest, chips):
    out_ref = rest[-1]
    rows = pq_ref.shape[1]
    mean = jnp.full((HEAD, HEAD), 1.0 / HEAD, BF16)
    for n in (0, 1):
        carried = carried_ref[n].astype(F32)
        for i in range(rows // CHUNK):
            r0 = i * CHUNK
            state = carried
            if i:
                state = st_ref[n, i - 1].astype(F32) + carried * gate_ref[chips + 7 + i : chips + 8 + i]
            held = jnp.dot(pq_ref[n, r0 : r0 + CHUNK], state.astype(BF16), preferred_element_type=F32)
            mixture = mix_ref[n, r0 : r0 + CHUNK].astype(F32) + held
            square = jnp.dot((mixture * mixture).astype(BF16), mean, preferred_element_type=F32)
            scale = lax.rsqrt(square + 1e-06) * gain_ref[0:1, n * HEAD : (n + 1) * HEAD]
            out_ref[r0 : r0 + CHUNK, n * HEAD : (n + 1) * HEAD] = (mixture * scale).astype(BF16)


def rim_kernel(q_ref, k_ref, v_ref, out_ref):
    out_ref[0] = q_ref[...]
    out_ref[1] = k_ref[...]
    out_ref[2] = v_ref[...]


def join_kernel(gate_ref, own_ref, got_ref, out_ref, *, chips):
    own, got = gate_ref[chips : chips + 1], gate_ref[chips + 1 : chips + 2]
    out_ref[...] = (own_ref[...].astype(F32) * own + got_ref[...].astype(F32) * got).astype(BF16)


def total_kernel(gate_ref, spread_ref, out_ref):
    total = jnp.zeros(out_ref.shape, F32)
    for z in range(spread_ref.shape[0]):
        total = total * gate_ref[z : z + 1] + spread_ref[z].astype(F32)
    out_ref[...] = total


def enter_kernel(gate_ref, spread_ref, near_ref, far_ref, out_ref):
    running = near_ref[...] + far_ref[...]
    for z in range(spread_ref.shape[0]):
        out_ref[z] = running.astype(BF16)
        running = running * gate_ref[z : z + 1] + spread_ref[z].astype(F32)


def carry_kernel(gate_ref, entered_ref, own_ref, got_ref, mine_ref, other_ref, *, chips):
    gate = [gate_ref[chips + 2 + n : chips + 3 + n] for n in range(4)]
    entered = entered_ref[...].astype(F32)
    mine_ref[...] = (entered * gate[0] + got_ref[...].astype(F32) * gate[1]).astype(BF16)
    other_ref[...] = (entered * gate[2] + own_ref[...].astype(F32) * gate[3]).astype(BF16)


def in_hbm(x):
    return pltpu.with_memory_space_constraint(x, pltpu.HBM)


def params(mib):
    return pltpu.CompilerParams(dimension_semantics=("arbitrary",), vmem_limit_bytes=mib * 1024 * 1024)


def small(kernel, outs, *args):
    return pl.pallas_call(
        kernel, out_shape=outs, compiler_params=pltpu.CompilerParams(vmem_limit_bytes=4 * 1024 * 1024)
    )(*args)


def shaped(*shape, dtype=BF16):
    return jax.ShapeDtypeStruct(shape, dtype)


def per_device(query_rows, key_rows, value_rows, lengths, conv_weight, out_gain):
    query_rows, key_rows, value_rows, conv_weight = (
        in_hbm(x) for x in (query_rows, key_rows, value_rows, conv_weight)
    )
    rows, channels = query_rows.shape
    heads = channels // HEAD
    pairs = heads // 2
    half = heads // 2
    chunks = rows // CHUNK
    chips, x_count = lax.axis_size("z"), lax.axis_size("x")
    ctx_count = x_count * chips * 2
    here = lax.axis_index(CTX).astype(jnp.int32).reshape(1)
    swap = [(0, 1), (1, 0)]

    smem = pl.BlockSpec(memory_space=pltpu.SMEM)
    last_rows = pl.BlockSpec((8, channels), lambda i: (rows // 8 - 1, 0))
    rims = pl.pallas_call(
        rim_kernel,
        grid=(1,),
        in_specs=[last_rows] * 3,
        out_specs=pl.BlockSpec((3, 8, channels), lambda i: (0, 0, 0)),
        out_shape=shaped(3, 8, channels),
        compiler_params=params(4),
        name="rim",
    )(query_rows, key_rows, value_rows)
    rims = lax.ppermute(rims, CTX, [(i, i + 1) for i in range(ctx_count - 1)])

    whole = lambda *shape: pl.BlockSpec(shape, lambda p, *s: (0,) * len(shape))
    column = lambda count: pl.BlockSpec((count, PAIR), lambda p: (0, p))
    taps = lambda w: pl.BlockSpec((None, 4, PAIR), lambda p: (w, 0, p))
    two = lambda *shape: pl.BlockSpec((2,) + shape, lambda p: (p,) + (0,) * len(shape))
    anywhere = pl.BlockSpec(memory_space=pl.ANY)
    lengths = lengths.reshape(1, -1)
    gate_rows = 24
    half_pairs = pairs // 2

    def masks(count):
        return [pltpu.VMEM((count + 8, HEAD), F32), pltpu.VMEM((3, count, HEAD), F32)]

    pk_late, val_late, st_late, gates = pl.pallas_call(
        lambda *refs: late_kernel(*refs, chips=chips),
        grid=(pairs,),
        in_specs=[smem, whole(1, HEAD), column(rows), column(rows), taps(1), taps(2)],
        out_specs=[
            two(rows - CHUNK, HEAD),
            two(rows - CHUNK, HEAD),
            two(chunks - 1, HEAD, HEAD),
            whole(gate_rows, HEAD),
        ],
        out_shape=[
            pltpu.HBM((heads, rows - CHUNK, HEAD), BF16),
            pltpu.HBM((heads, rows - CHUNK, HEAD), BF16),
            shaped(heads, chunks - 1, HEAD, HEAD, dtype=F32),
            shaped(gate_rows, HEAD, dtype=F32),
        ],
        scratch_shapes=masks(rows) + [pltpu.VMEM((2, rows + 8, HEAD), F32)] * 2,
        compiler_params=params(20),
        name="late",
    )(here, lengths, key_rows, value_rows, conv_weight, conv_weight)
    pk_late, val_late = in_hbm(pk_late), in_hbm(val_late)

    def by_core(mine):
        pair = lambda p, s: p + ((s[0] % 2) if mine else (1 - s[0] % 2)) * half_pairs
        part = lambda *shape: pl.BlockSpec((2,) + shape, lambda p, s: (pair(p, s),) + (0,) * len(shape))
        cols = lambda count: pl.BlockSpec((count, PAIR), lambda p, s: (0, pair(p, s)))
        lead = lambda w, count: pl.BlockSpec((None, count, PAIR), lambda p, s: (w, 0, pair(p, s)))
        return part, cols, lead

    plain = lambda *shape: pl.BlockSpec((2,) + shape, lambda p, s: (p,) + (0,) * len(shape))

    def first(mine, *so_far):
        part, cols, lead = by_core(mine)
        args = (here, lengths, gates, key_rows, value_rows, rims, rims, conv_weight, conv_weight, st_late)
        return pl.pallas_call(
            lambda *refs: first_kernel(*refs, rows=rows, chips=chips),
            grid_spec=pltpu.PrefetchScalarGridSpec(
                num_scalar_prefetch=1,
                grid=(half_pairs,),
                in_specs=[
                    whole(1, HEAD),
                    whole(gate_rows, HEAD),
                    cols(CHUNK),
                    cols(CHUNK),
                    lead(1, 8),
                    lead(2, 8),
                    lead(1, 4),
                    lead(2, 4),
                    part(chunks - 1, HEAD, HEAD),
                ]
                + [anywhere] * len(so_far),
                out_specs=[
                    part(CHUNK, HEAD),
                    part(CHUNK, HEAD),
                    part(chunks - 1, HEAD, HEAD),
                    plain(HEAD, HEAD),
                ],
                scratch_shapes=masks(CHUNK) + [pltpu.VMEM((2, CHUNK + 8, HEAD), F32)] * 2,
            ),
            out_shape=[
                pltpu.HBM((heads, CHUNK, HEAD), BF16),
                pltpu.HBM((heads, CHUNK, HEAD), BF16),
                pltpu.HBM((heads, chunks - 1, HEAD, HEAD), BF16),
                shaped(half, HEAD, HEAD),
            ],
            input_output_aliases={len(args) + n: n for n in range(len(so_far))},
            compiler_params=params(8),
            name="first",
        )(*args, *so_far)

    *so_far, other = first(False)
    so_far = [in_hbm(x) for x in so_far]
    got = lax.ppermute(other, "c", swap)
    pk_first, val_first, inner, own = first(True, *so_far)
    pk_first, val_first, inner = in_hbm(pk_first), in_hbm(val_first), in_hbm(inner)

    state = (half, HEAD, HEAD)
    chip_tail = small(lambda *r: join_kernel(*r, chips=chips), pltpu.HBM(state, BF16), gates, own, got)
    spread = lax.all_to_all(chip_tail.reshape(chips, -1, HEAD), "z", 0, 0, tiled=True)

    def attend(pair, count, *so_far):
        at = lambda p: p + pair
        cols = lambda n: pl.BlockSpec((n, PAIR), lambda p: (0, at(p)))
        part = lambda *shape: pl.BlockSpec((2,) + shape, lambda p: (at(p),) + (0,) * len(shape))
        args = (here, lengths, query_rows, rims, conv_weight, pk_first, pk_late, val_first, val_late)
        return pl.pallas_call(
            attend_kernel,
            grid=(count,),
            in_specs=[
                smem,
                whole(1, HEAD),
                cols(rows),
                pl.BlockSpec((None, 8, PAIR), lambda p: (0, 0, at(p))),
                pl.BlockSpec((None, 4, PAIR), lambda p: (0, 0, at(p))),
                part(CHUNK, HEAD),
                part(rows - CHUNK, HEAD),
                part(CHUNK, HEAD),
                part(rows - CHUNK, HEAD),
            ]
            + [anywhere] * len(so_far),
            out_specs=[part(rows, HEAD), part(rows, HEAD)],
            out_shape=[pltpu.HBM((heads, rows, HEAD), BF16)] * 2,
            scratch_shapes=masks(rows)
            + [pltpu.VMEM((2, rows + 8, HEAD), F32), pltpu.VMEM((chunks, CHUNK, CHUNK), BF16)],
            input_output_aliases={len(args) + n: n for n in range(len(so_far))},
            compiler_params=params(20),
            name="attend",
        )(*args, *so_far)

    mixed = [in_hbm(x) for x in attend(0, half_pairs)]
    phi_q, mix = (in_hbm(x) for x in attend(half_pairs, half_pairs, *mixed))

    row_total = small(total_kernel, shaped(*spread.shape[1:], dtype=F32), gates, spread)
    far = lax.ppermute(row_total, "x", [(1, 3)])
    near = lax.ppermute(row_total, "x", [(i, i + 1) for i in range(x_count - 1)])
    entering = small(enter_kernel, pltpu.HBM(spread.shape, BF16), gates, spread, near, far)
    entered = lax.all_to_all(entering, "z", 0, 0, tiled=True).reshape(state)
    carried_own, carried_other = small(
        lambda *r: carry_kernel(*r, chips=chips), [shaped(*state)] * 2, gates, entered, own, got
    )
    carried_far = lax.ppermute(carried_other, "c", swap)

    def finish(mine, carried, *so_far):
        part, cols, _ = by_core(mine)
        args = (here, gates, mix, phi_q, inner, carried, out_gain.reshape(1, -1))
        return pl.pallas_call(
            lambda *refs: finish_kernel(*refs, chips=chips),
            grid_spec=pltpu.PrefetchScalarGridSpec(
                num_scalar_prefetch=1,
                grid=(half_pairs,),
                in_specs=[
                    whole(gate_rows, HEAD),
                    part(rows, HEAD),
                    part(rows, HEAD),
                    part(chunks - 1, HEAD, HEAD),
                    plain(HEAD, HEAD),
                    cols(1),
                ]
                + [anywhere] * len(so_far),
                out_specs=cols(rows),
            ),
            out_shape=shaped(rows, channels),
            input_output_aliases={len(args) + n: n for n in range(len(so_far))},
            compiler_params=params(16),
            name="finish",
        )(*args, *so_far)

    done = finish(True, carried_own)
    return finish(False, carried_far, done)


def solution(mesh):
    finer = Mesh(mesh.devices.reshape(mesh.shape["dp"], 4, 8, 2), DP_CTX)

    return jax.shard_map(
        per_device,
        mesh=finer,
        in_specs=(P(DP_CTX, None), P(DP_CTX, None), P(DP_CTX, None), P("dp"), P(), P()),
        out_specs=P(DP_CTX, None),
        check_vma=False,
    )
```

```python
import jax
import jax.numpy as jnp
from jax import lax
from jax.experimental import pallas as pl
from jax.experimental.pallas import tpu as pltpu
from jax.sharding import Mesh
from jax.sharding import PartitionSpec as P

HEAD = 128
CHUNK = 256
GROUP = 16
CTX = ("x", "z", "c")
DP_CTX = ("dp", "x", "z", "c")
F32 = jnp.float32
BF16 = jnp.bfloat16


def one_if(flag):
    return jnp.where(flag, 1.0, 0.0)


def starts_of(lengths):
    rows = jnp.broadcast_to(lengths, (8, HEAD))
    before = one_if(
        lax.broadcasted_iota(jnp.int32, (HEAD, HEAD), 0) < lax.broadcasted_iota(jnp.int32, (HEAD, HEAD), 1)
    ).astype(BF16)
    high = jnp.dot((rows >> 8).astype(F32).astype(BF16), before, preferred_element_type=F32)
    low = jnp.dot((rows & 255).astype(F32).astype(BF16), before, preferred_element_type=F32)
    return high * 256.0 + low


def docs_of(positions, starts):
    below = one_if(starts[0:1] <= positions.astype(F32)).astype(BF16)
    return jnp.dot(below, jnp.ones((HEAD, HEAD), BF16), preferred_element_type=F32), below


def wide(rows):
    return jnp.concatenate([rows, rows], axis=1)


def fill_doc(first, starts, doc_s, m_s):
    count = m_s.shape[1]
    iota = lax.broadcasted_iota(jnp.int32, (count + 8, HEAD), 0)
    doc, below = docs_of(iota + (first - 8), starts)
    doc_s[...] = doc
    for j in (1, 2, 3):
        m_s[j - 1] = one_if(doc_s[8 - j : 8 - j + count] == doc_s[8:])
    return below


def conv(ext, taps, m_s, r0):
    acc = taps[0:1] * ext[8 + r0 : 8 + r0 + CHUNK]
    for j in (1, 2, 3):
        acc += taps[j : j + 1] * (ext[8 + r0 - j : 8 + r0 - j + CHUNK] * m_s[j - 1, r0 : r0 + CHUNK])
    return acc


def silu_of_half(half):
    return half * jnp.tanh(half) + half


def fill_live(doc, live_s):
    for r0 in range(0, live_s.shape[0], CHUNK):
        last = doc[8 + r0 + CHUNK - 1 : 8 + r0 + CHUNK]
        live_s[r0 : r0 + CHUNK] = one_if(doc[8 + r0 : 8 + r0 + CHUNK] == last).astype(BF16)


def kv_chunk(ext_k, ext_v, kw, vw, m_s, live_s, r0):
    key = silu_of_half(conv(ext_k, kw, m_s, r0)).astype(BF16)
    val = conv(ext_v, vw, m_s, r0).astype(BF16)
    live = live_s[r0 : r0 + CHUNK]
    tail = lax.dot_general(key * live, val, (((0,), (0,)), ((), ())), preferred_element_type=F32)
    return key, val, tail


def lanes(head, count=1):
    return pl.ds(pl.multiple_of(head * HEAD, HEAD), count * HEAD)


def run(copies):
    for copy in copies:
        copy.start()


def finish_all(copies):
    for copy in copies:
        copy.wait()


def late_kernel(
    here_ref, len_ref, k_hbm, v_hbm, w_ref,
    pk_hbm, val_hbm, st_ref, gate_ref, k0_ref, v0_ref,
    doc_s, m_s, live_s, ext_k, ext_v, kb, vb, pkb, valb, in_sem, out_sem, edge_sem,
    *, chips,
):
    rows = k_hbm.shape[0]
    chunks = rows // CHUNK
    pairs = kb.shape[0]
    tail_rows = pl.ds(CHUNK - GROUP, rows - CHUNK + GROUP)

    def fetch(p):
        cols = lanes(2 * p, 2)
        return [
            pltpu.make_async_copy(k_hbm.at[tail_rows, cols], kb.at[p], in_sem.at[0, p]),
            pltpu.make_async_copy(v_hbm.at[tail_rows, cols], vb.at[p], in_sem.at[1, p]),
        ]

    def store(p):
        two = pl.ds(2 * p, 2)
        return [
            pltpu.make_async_copy(pkb.at[two], pk_hbm.at[two], out_sem.at[0, p]),
            pltpu.make_async_copy(valb.at[two], val_hbm.at[two], out_sem.at[1, p]),
        ]

    edges = [
        pltpu.make_async_copy(k_hbm.at[pl.ds(0, CHUNK)], k0_ref, edge_sem.at[0]),
        pltpu.make_async_copy(v_hbm.at[pl.ds(0, CHUNK)], v0_ref, edge_sem.at[1]),
    ]
    for p in range(pairs):
        run(fetch(p))
    run(edges)

    here = here_ref[0]
    core = here % 2
    offset = here * rows
    starts = starts_of(len_ref[...])
    fill_doc(offset, starts, doc_s, m_s)
    fill_live(doc_s, live_s)
    chip = offset - core * rows
    first = (here // (2 * chips)) * (2 * chips * rows)
    mark = lax.broadcasted_iota(jnp.int32, (16, HEAD), 0)
    ends, _ = docs_of(first + mark * (2 * rows) - 1, starts)
    mine, _ = docs_of(chip + mark * rows - 1, starts)
    inner, _ = docs_of(offset + mark * CHUNK - 1, starts)
    keep_first = one_if(mine[1:2] == mine[0:1])
    keep_second = one_if(mine[2:3] == mine[1:2])
    second = jnp.full((1, HEAD), core, jnp.int32) == 1
    gate_ref[0:chips] = one_if(ends[1 : chips + 1] == ends[0:chips])
    one, zero = jnp.ones((1, HEAD), F32), jnp.zeros((1, HEAD), F32)
    rest = [
        jnp.where(second, one, keep_second),
        jnp.where(second, keep_second, one),
        jnp.where(second, keep_first, one),
        jnp.where(second, one, zero),
        jnp.where(second, one, keep_first),
        jnp.where(second, zero, one),
    ]
    for n, row in enumerate(rest):
        gate_ref[chips + n : chips + n + 1] = row
    for i in range(1, chunks):
        gate_ref[chips + 7 + i : chips + 8 + i] = one_if(inner[i : i + 1] == inner[0:1])
    for i in range(2, chunks + 1):
        gate_ref[chips + 9 + i : chips + 10 + i] = one_if(inner[i : i + 1] == inner[1:2])

    @pl.loop(0, pairs)
    def _(p):
        finish_all(fetch(p))
        for n in (0, 1):
            cols = slice(n * HEAD, (n + 1) * HEAD)
            ext_k[n, CHUNK - 8 :] = kb[p, :, cols].astype(F32)
            ext_v[n, CHUNK - 8 :] = vb[p, :, cols].astype(F32)
        taps = [(0.5 * w_ref[1, :, lanes(2 * p + n)], w_ref[2, :, lanes(2 * p + n)]) for n in (0, 1)]
        states = [jnp.zeros((HEAD, HEAD), F32)] * 2
        for i in range(1, chunks):
            r0 = i * CHUNK
            same = one_if(doc_s[8 + r0 - 1 : 8 + r0] == doc_s[8 + r0 + CHUNK - 1 : 8 + r0 + CHUNK])
            for n in (0, 1):
                key, val, tail = kv_chunk(ext_k.at[n], ext_v.at[n], *taps[n], m_s, live_s, r0)
                pkb[2 * p + n, r0 - CHUNK : r0] = key
                valb[2 * p + n, r0 - CHUNK : r0] = val
                states[n] = states[n] * same + tail
                st_ref[2 * p + n, i - 1] = states[n]
        run(store(p))

    finish_all(edges)
    for p in range(pairs):
        finish_all(store(p))


def first_kernel(
    here_ref, len_ref, gate_ref, k_ref, v_ref, rim_ref, w_ref, late_ref,
    pk_ref, val_ref, st_ref, tail_ref, doc_s, m_s, live_s, ext_k, ext_v,
    *, mine, rows, chips,
):
    heads = pk_ref.shape[0]
    here = here_ref[0]
    base = (here % 2 if mine else 1 - here % 2) * heads
    count = late_ref.shape[1] + 1
    fill_doc(here * rows, starts_of(len_ref[...]), doc_s, m_s)
    fill_live(doc_s, live_s)

    @pl.loop(0, heads // 2)
    def _(p):
        for n in (0, 1):
            cols = lanes(base + 2 * p + n)
            ext_k[n, 0:8] = rim_ref[1, :, cols].astype(F32)
            ext_v[n, 0:8] = rim_ref[2, :, cols].astype(F32)
            ext_k[n, 8:] = k_ref[:, cols].astype(F32)
            ext_v[n, 8:] = v_ref[:, cols].astype(F32)
        for n in (0, 1):
            h = 2 * p + n
            cols = lanes(base + h)
            key, val, tail = kv_chunk(
                ext_k.at[n], ext_v.at[n], 0.5 * w_ref[1, :, cols], w_ref[2, :, cols], m_s, live_s, 0
            )
            pk_ref[h] = key
            val_ref[h] = val
            st_ref[h, 0] = tail.astype(BF16)
            for i in range(1, count):
                state = late_ref[base + h, i - 1] + tail * gate_ref[chips + 10 + i : chips + 11 + i]
                if i < count - 1:
                    st_ref[h, i] = state.astype(BF16)
            tail_ref[h] = state.astype(BF16)


def attend_kernel(
    here_ref, len_ref, q_hbm, pkl_hbm, vall_hbm, pkf_ref, valf_ref, rim_ref, w_ref,
    pq_out, mix_out, doc_s, m_s, use_s, ext, allow_s, qb, kb, vb, in_sem, *staging,
    mine,
):
    heads, rows, _ = pq_out.shape
    chunks = rows // CHUNK
    pairs = heads // 2
    here = here_ref[0]
    base = (here % 2 if mine else 1 - here % 2) * heads
    pq_ref, mix_ref = staging[:2] if staging else (pq_out, mix_out)

    def fetch(p):
        two = pl.ds(base + 2 * p, 2)
        return [
            pltpu.make_async_copy(q_hbm.at[:, lanes(base + 2 * p, 2)], qb.at[p], in_sem.at[0, p]),
            pltpu.make_async_copy(pkl_hbm.at[two], kb.at[p], in_sem.at[1, p]),
            pltpu.make_async_copy(vall_hbm.at[two], vb.at[p], in_sem.at[2, p]),
        ]

    def store(p):
        two = pl.ds(2 * p, 2)
        return [
            pltpu.make_async_copy(pq_ref.at[two], pq_out.at[two], staging[2].at[0, p]),
            pltpu.make_async_copy(mix_ref.at[two], mix_out.at[two], staging[2].at[1, p]),
        ]

    for p in range(pairs):
        run(fetch(p))

    below = fill_doc(here * rows, starts_of(len_ref[...]), doc_s, m_s)
    across = lax.dot_general(
        jnp.ones((8, HEAD), BF16), below[8:], (((1,), (1,)), ((), ())), preferred_element_type=F32
    )
    causal = lax.broadcasted_iota(jnp.int32, (CHUNK, CHUNK), 1) <= lax.broadcasted_iota(
        jnp.int32, (CHUNK, CHUNK), 0
    )
    for i in range(chunks):
        r0 = i * CHUNK
        doc = doc_s[8 + r0 : 8 + r0 + CHUNK]
        same = wide(doc) == across[0:1, r0 : r0 + CHUNK]
        allow_s[i] = jnp.where(same & causal, 1.0, 0.0).astype(BF16)
        use_s[r0 : r0 + CHUNK] = one_if(doc == doc_s[8 + r0 - 1 : 8 + r0]).astype(BF16)

    @pl.loop(0, pairs)
    def _(p):
        finish_all(fetch(p))
        for n in (0, 1):
            ext[n, 0:8] = rim_ref[0, :, lanes(base + 2 * p + n)].astype(F32)
            ext[n, 8:] = qb[p, :, n * HEAD : (n + 1) * HEAD].astype(F32)
        taps = [0.5 * w_ref[0, :, lanes(base + 2 * p + n)] for n in (0, 1)]

        def make(i, n):
            rows = slice(i * CHUNK, (i + 1) * CHUNK)
            query = silu_of_half(conv(ext.at[n], taps[n], m_s, i * CHUNK)).astype(BF16)
            pq_ref[2 * p + n, rows] = query * use_s[rows]
            return query

        def mixed(i, n, query):
            r0 = i * CHUNK
            key = pkf_ref[2 * p + n] if i == 0 else kb[p, n, r0 - CHUNK : r0]
            val = valf_ref[2 * p + n] if i == 0 else vb[p, n, r0 - CHUNK : r0]
            scores = lax.dot_general(query, key, (((1,), (1,)), ((), ())), preferred_element_type=F32)
            weights = scores.astype(BF16) * allow_s[i]
            mix = jnp.dot(weights, val, preferred_element_type=F32)
            mix_ref[2 * p + n, r0 : r0 + CHUNK] = mix.astype(BF16)

        ahead = None
        for i in range(chunks):
            for n in (0, 1):
                query = make(i, n)
                if ahead is not None:
                    mixed(*ahead)
                ahead = (i, n, query)
        mixed(*ahead)
        if staging:
            run(store(p))

    if staging:
        for p in range(pairs):
            finish_all(store(p))


def finish_kernel(here_ref, gate_ref, pq_ref, mix_ref, st_ref, carried_ref, gain_ref, *rest, mine, chips):
    if mine:
        pqx_hbm, mixx_hbm, out_hbm, pqx_ref, mixx_ref, outb, out_sem, next_sem = rest
        onward = [
            pltpu.make_async_copy(pqx_hbm, pqx_ref, next_sem.at[0]),
            pltpu.make_async_copy(mixx_hbm, mixx_ref, next_sem.at[1]),
        ]
    else:
        _, out_hbm, outb, out_sem = rest
        onward = []
    heads, rows, _ = pq_ref.shape
    chunks = rows // CHUNK
    base = (here_ref[0] % 2 if mine else 1 - here_ref[0] % 2) * heads
    mean = jnp.full((HEAD, HEAD), 1.0 / HEAD, BF16)
    run(onward)

    def store(p, i):
        rows = pl.ds(i * CHUNK, CHUNK)
        return pltpu.make_async_copy(
            outb.at[p, rows], out_hbm.at[rows, lanes(base + 2 * p, 2)], out_sem.at[p, i]
        )

    @pl.loop(0, heads // 2)
    def _(p):
        gain = [gain_ref[:, lanes(base + 2 * p + n)] for n in (0, 1)]

        def blend(i, n):
            h = 2 * p + n
            state = carried_ref[h].astype(F32)
            if i:
                state = st_ref[h, i - 1].astype(F32) + state * gate_ref[chips + 7 + i : chips + 8 + i]
            rows = slice(i * CHUNK, (i + 1) * CHUNK)
            held = jnp.dot(pq_ref[h, rows], state.astype(BF16), preferred_element_type=F32)
            return mix_ref[h, rows].astype(F32) + held

        def norm(i, n, mixture):
            square = jnp.dot((mixture * mixture).astype(BF16), mean, preferred_element_type=F32)
            scale = lax.rsqrt(square + 1e-06) * gain[n]
            outb[p, i * CHUNK : (i + 1) * CHUNK, n * HEAD : (n + 1) * HEAD] = (mixture * scale).astype(BF16)
            if n:
                store(p, i).start()

        ahead = None
        for i in range(chunks):
            for n in (0, 1):
                mixture = blend(i, n)
                if ahead is not None:
                    norm(*ahead)
                ahead = (i, n, mixture)
        norm(*ahead)

    finish_all(onward)
    for p in range(heads // 2):
        for i in range(chunks):
            store(p, i).wait()


def rim_kernel(q_ref, k_ref, v_ref, out_ref):
    out_ref[0] = q_ref[...]
    out_ref[1] = k_ref[...]
    out_ref[2] = v_ref[...]


def join_kernel(gate_ref, own_ref, got_ref, out_ref, *, chips):
    own, got = gate_ref[chips : chips + 1], gate_ref[chips + 1 : chips + 2]
    out_ref[...] = (own_ref[...].astype(F32) * own + got_ref[...].astype(F32) * got).astype(BF16)


def total_kernel(gate_ref, spread_ref, out_ref):
    total = jnp.zeros(out_ref.shape, F32)
    for z in range(spread_ref.shape[0]):
        total = total * gate_ref[z : z + 1] + spread_ref[z].astype(F32)
    out_ref[...] = total


def enter_kernel(gate_ref, spread_ref, near_ref, far_ref, out_ref):
    running = near_ref[...] + far_ref[...]
    for z in range(spread_ref.shape[0]):
        out_ref[z] = running.astype(BF16)
        running = running * gate_ref[z : z + 1] + spread_ref[z].astype(F32)


def carry_kernel(gate_ref, entered_ref, own_ref, got_ref, mine_ref, other_ref, *, chips):
    gate = [gate_ref[chips + 2 + n : chips + 3 + n] for n in range(4)]
    entered = entered_ref[...].astype(F32)
    mine_ref[...] = (entered * gate[0] + got_ref[...].astype(F32) * gate[1]).astype(BF16)
    other_ref[...] = (entered * gate[2] + own_ref[...].astype(F32) * gate[3]).astype(BF16)


def in_hbm(x):
    return pltpu.with_memory_space_constraint(x, pltpu.HBM)


def params(mib):
    return pltpu.CompilerParams(vmem_limit_bytes=mib * 1024 * 1024)


def small(kernel, outs, *args):
    return pl.pallas_call(
        kernel, out_shape=outs, compiler_params=pltpu.CompilerParams(vmem_limit_bytes=4 * 1024 * 1024)
    )(*args)


def shaped(*shape, dtype=BF16):
    return jax.ShapeDtypeStruct(shape, dtype)


def per_device(query_rows, key_rows, value_rows, lengths, conv_weight, out_gain):
    query_rows, key_rows, value_rows = (in_hbm(x) for x in (query_rows, key_rows, value_rows))
    rows, channels = query_rows.shape
    heads = channels // HEAD
    half = heads // 2
    chunks = rows // CHUNK
    chips, x_count = lax.axis_size("z"), lax.axis_size("x")
    ctx_count = x_count * chips * 2
    here = lax.axis_index(CTX).astype(jnp.int32).reshape(1)
    swap = [(0, 1), (1, 0)]

    smem = pl.BlockSpec(memory_space=pltpu.SMEM)
    last_rows = pl.BlockSpec((8, channels), lambda i: (rows // 8 - 1, 0))
    rims = pl.pallas_call(
        rim_kernel,
        grid=(1,),
        in_specs=[last_rows] * 3,
        out_specs=pl.BlockSpec((3, 8, channels), lambda i: (0, 0, 0)),
        out_shape=shaped(3, 8, channels),
        compiler_params=params(4),
        name="rim",
    )(query_rows, key_rows, value_rows)
    rims = lax.ppermute(rims, CTX, [(i, i + 1) for i in range(ctx_count - 1)])

    vmem = pl.BlockSpec(memory_space=pltpu.VMEM)
    hbm = pl.BlockSpec(memory_space=pl.ANY)
    lengths = lengths.reshape(1, -1)
    gains = out_gain.reshape(1, -1)
    gate_rows = 24
    pairs, half_pairs = heads // 2, half // 2
    later = rows - CHUNK
    dma = lambda *shape: pltpu.SemaphoreType.DMA(shape)

    def masks(count):
        return [
            pltpu.VMEM((count + 8, HEAD), F32),
            pltpu.VMEM((3, count, HEAD), F32),
            pltpu.VMEM((count, HEAD), BF16),
        ]

    pk_late, val_late, st_late, gates, key_head, value_head = pl.pallas_call(
        lambda *refs: late_kernel(*refs, chips=chips),
        in_specs=[smem, vmem, hbm, hbm, vmem],
        out_specs=[hbm, hbm, vmem, vmem, vmem, vmem],
        out_shape=[
            pltpu.HBM((heads, later, HEAD), BF16),
            pltpu.HBM((heads, later, HEAD), BF16),
            shaped(heads, chunks - 1, HEAD, HEAD, dtype=F32),
            shaped(gate_rows, HEAD, dtype=F32),
            shaped(CHUNK, channels),
            shaped(CHUNK, channels),
        ],
        scratch_shapes=masks(rows)
        + [pltpu.VMEM((2, rows + 8, HEAD), F32)] * 2
        + [pltpu.VMEM((pairs, later + GROUP, 2 * HEAD), BF16)] * 2
        + [pltpu.VMEM((heads, later, HEAD), BF16)] * 2
        + [dma(2, pairs), dma(2, pairs), dma(2)],
        compiler_params=params(20),
        name="late",
    )(here, lengths, key_rows, value_rows, conv_weight)
    pk_late, val_late = in_hbm(pk_late), in_hbm(val_late)

    def first(mine):
        return pl.pallas_call(
            lambda *refs: first_kernel(*refs, mine=mine, rows=rows, chips=chips),
            in_specs=[smem] + [vmem] * 7,
            out_specs=[vmem] * 4,
            out_shape=[
                shaped(half, CHUNK, HEAD),
                shaped(half, CHUNK, HEAD),
                shaped(half, chunks - 1, HEAD, HEAD),
                shaped(half, HEAD, HEAD),
            ],
            scratch_shapes=masks(CHUNK) + [pltpu.VMEM((2, CHUNK + 8, HEAD), F32)] * 2,
            compiler_params=params(8),
            name="first",
        )(here, lengths, gates, key_head, value_head, rims, conv_weight, st_late)

    pk_other, val_other, inner_other, other = first(False)
    got = lax.ppermute(other, "c", swap)
    pk_own, val_own, inner_own, own = first(True)

    state = (half, HEAD, HEAD)
    chip_tail = small(lambda *r: join_kernel(*r, chips=chips), pltpu.HBM(state, BF16), gates, own, got)
    spread = lax.all_to_all(chip_tail.reshape(chips, -1, HEAD), "z", 0, 0, tiled=True)

    def attend(mine, pk_first, val_first):
        shape = (half, rows, HEAD)
        return pl.pallas_call(
            lambda *refs: attend_kernel(*refs, mine=mine),
            in_specs=[smem, vmem, hbm, hbm, hbm, vmem, vmem, vmem, vmem],
            out_specs=[vmem if mine else hbm] * 2,
            out_shape=[shaped(*shape) if mine else pltpu.HBM(shape, BF16)] * 2,
            scratch_shapes=masks(rows)
            + [pltpu.VMEM((2, rows + 8, HEAD), F32), pltpu.VMEM((chunks, CHUNK, CHUNK), BF16)]
            + [pltpu.VMEM((half_pairs, rows, 2 * HEAD), BF16)]
            + [pltpu.VMEM((half_pairs, 2, later, HEAD), BF16)] * 2
            + [dma(3, half_pairs)]
            + ([] if mine else [pltpu.VMEM(shape, BF16)] * 2 + [dma(2, half_pairs)]),
            compiler_params=params(24),
            name="attend",
        )(here, lengths, query_rows, pk_late, val_late, pk_first, val_first, rims, conv_weight)

    phi_other, mix_other = (in_hbm(x) for x in attend(False, pk_other, val_other))
    phi_own, mix_own = attend(True, pk_own, val_own)

    row_total = small(total_kernel, shaped(*spread.shape[1:], dtype=F32), gates, spread)
    far = lax.ppermute(row_total, "x", [(1, 3)])
    near = lax.ppermute(row_total, "x", [(i, i + 1) for i in range(x_count - 1)])
    entering = small(enter_kernel, pltpu.HBM(spread.shape, BF16), gates, spread, near, far)
    entered = lax.all_to_all(entering, "z", 0, 0, tiled=True).reshape(state)
    carried_own, carried_other = small(
        lambda *r: carry_kernel(*r, chips=chips), [shaped(*state)] * 2, gates, entered, own, got
    )
    carried_far = lax.ppermute(carried_other, "c", swap)

    def finish(mine, phi, mix, inner, carried, *others):
        shape = (half, rows, HEAD)
        ahead = [shaped(*shape)] * 2 if mine else []
        args = (here, gates, phi, mix, inner, carried, gains, *others)
        return pl.pallas_call(
            lambda *refs: finish_kernel(*refs, mine=mine, chips=chips),
            in_specs=[smem] + [vmem] * 6 + [hbm] * len(others),
            out_specs=[hbm] + [vmem] * len(ahead),
            out_shape=[pltpu.HBM((rows, channels), BF16)] + ahead,
            scratch_shapes=[pltpu.VMEM((half_pairs, rows, 2 * HEAD), BF16), dma(half_pairs, chunks)]
            + ([dma(2)] if mine else []),
            input_output_aliases={} if mine else {len(args) - 1: 0},
            compiler_params=params(12),
            name="finish",
        )(*args)

    done, phi_other, mix_other = finish(
        True, phi_own, mix_own, inner_own, carried_own, phi_other, mix_other
    )
    return finish(False, phi_other, mix_other, inner_other, carried_far, done)[0]


def solution(mesh):
    finer = Mesh(mesh.devices.reshape(mesh.shape["dp"], 4, 8, 2), DP_CTX)

    return jax.shard_map(
        per_device,
        mesh=finer,
        in_specs=(P(DP_CTX, None), P(DP_CTX, None), P(DP_CTX, None), P("dp"), P(), P()),
        out_specs=P(DP_CTX, None),
        check_vma=False,
    )
```

```python
import jax
import jax.numpy as jnp
from jax import lax
from jax.experimental import pallas as pl
from jax.experimental.pallas import tpu as pltpu
from jax.sharding import Mesh
from jax.sharding import PartitionSpec as P

HEAD = 128
CHUNK = 256
GROUP = 16
CTX = ("x", "z", "c")
DP_CTX = ("dp", "x", "z", "c")
F32 = jnp.float32
BF16 = jnp.bfloat16


def one_if(flag):
    return jnp.where(flag, 1.0, 0.0)


def starts_of(lengths):
    rows = jnp.broadcast_to(lengths, (8, HEAD))
    before = one_if(
        lax.broadcasted_iota(jnp.int32, (HEAD, HEAD), 0) < lax.broadcasted_iota(jnp.int32, (HEAD, HEAD), 1)
    ).astype(BF16)
    high = jnp.dot((rows >> 8).astype(F32).astype(BF16), before, preferred_element_type=F32)
    low = jnp.dot((rows & 255).astype(F32).astype(BF16), before, preferred_element_type=F32)
    return high * 256.0 + low


def docs_of(positions, starts):
    below = one_if(starts[0:1] <= positions.astype(F32)).astype(BF16)
    return jnp.dot(below, jnp.ones((HEAD, HEAD), BF16), preferred_element_type=F32), below


def wide(rows):
    return jnp.concatenate([rows, rows], axis=1)


def fill_doc(first, starts, doc_s, m_s):
    count = m_s.shape[1]
    iota = lax.broadcasted_iota(jnp.int32, (count + 8, HEAD), 0)
    doc, below = docs_of(iota + (first - 8), starts)
    doc_s[...] = doc
    for j in (1, 2, 3):
        m_s[j - 1] = one_if(doc_s[8 - j : 8 - j + count] == doc_s[8:])
    return below


def conv(ext, taps, m_s, r0):
    acc = taps[0:1] * ext[8 + r0 : 8 + r0 + CHUNK]
    for j in (1, 2, 3):
        acc += taps[j : j + 1] * (ext[8 + r0 - j : 8 + r0 - j + CHUNK] * m_s[j - 1, r0 : r0 + CHUNK])
    return acc


def silu_of_half(half):
    return half * jnp.tanh(half) + half


def fill_live(doc, live_s):
    for r0 in range(0, live_s.shape[0], CHUNK):
        last = doc[8 + r0 + CHUNK - 1 : 8 + r0 + CHUNK]
        live_s[r0 : r0 + CHUNK] = one_if(doc[8 + r0 : 8 + r0 + CHUNK] == last).astype(BF16)


def kv_chunk(ext_k, ext_v, kw, vw, m_s, live_s, r0):
    key = silu_of_half(conv(ext_k, kw, m_s, r0)).astype(BF16)
    val = conv(ext_v, vw, m_s, r0).astype(BF16)
    live = live_s[r0 : r0 + CHUNK]
    tail = lax.dot_general(key * live, val, (((0,), (0,)), ((), ())), preferred_element_type=F32)
    return key, val, tail


def lanes(head, count=1):
    return pl.ds(pl.multiple_of(head * HEAD, HEAD), count * HEAD)


def run(copies):
    for copy in copies:
        copy.start()


def finish_all(copies):
    for copy in copies:
        copy.wait()


def late_kernel(
    here_ref, len_ref, k_hbm, v_hbm, w_ref,
    pk_hbm, val_hbm, st_ref, gate_ref, k0_ref, v0_ref,
    doc_s, m_s, live_s, ext_k, ext_v, kb, vb, pkb, valb, in_sem, out_sem, edge_sem,
    *, chips,
):
    rows = k_hbm.shape[0]
    chunks = rows // CHUNK
    pairs = kb.shape[0]
    tail_rows = pl.ds(CHUNK - GROUP, rows - CHUNK + GROUP)

    def fetch(p):
        cols = lanes(2 * p, 2)
        return [
            pltpu.make_async_copy(k_hbm.at[tail_rows, cols], kb.at[p], in_sem.at[0, p]),
            pltpu.make_async_copy(v_hbm.at[tail_rows, cols], vb.at[p], in_sem.at[1, p]),
        ]

    def store(p):
        two = pl.ds(2 * p, 2)
        return [
            pltpu.make_async_copy(pkb.at[two], pk_hbm.at[two], out_sem.at[0, p]),
            pltpu.make_async_copy(valb.at[two], val_hbm.at[two], out_sem.at[1, p]),
        ]

    edges = [
        pltpu.make_async_copy(k_hbm.at[pl.ds(0, CHUNK)], k0_ref, edge_sem.at[0]),
        pltpu.make_async_copy(v_hbm.at[pl.ds(0, CHUNK)], v0_ref, edge_sem.at[1]),
    ]
    for p in range(pairs):
        run(fetch(p))
    run(edges)

    here = here_ref[0]
    core = here % 2
    offset = here * rows
    starts = starts_of(len_ref[...])
    fill_doc(offset, starts, doc_s, m_s)
    fill_live(doc_s, live_s)
    chip = offset - core * rows
    chip_mark = lax.broadcasted_iota(jnp.int32, (chips + 8, HEAD), 0)
    mark = lax.broadcasted_iota(jnp.int32, (16, HEAD), 0)
    ends, _ = docs_of(chip_mark * (2 * rows) - 1, starts)
    mine, _ = docs_of(chip + mark * rows - 1, starts)
    inner, _ = docs_of(offset + mark * CHUNK - 1, starts)
    keep_first = one_if(mine[1:2] == mine[0:1])
    keep_second = one_if(mine[2:3] == mine[1:2])
    second = jnp.full((1, HEAD), core, jnp.int32) == 1
    gate_ref[0:chips] = one_if(ends[1 : chips + 1] == ends[0:chips])
    one, zero = jnp.ones((1, HEAD), F32), jnp.zeros((1, HEAD), F32)
    rest = [
        jnp.where(second, one, keep_second),
        jnp.where(second, keep_second, one),
        jnp.where(second, keep_first, one),
        jnp.where(second, one, zero),
        jnp.where(second, one, keep_first),
        jnp.where(second, zero, one),
    ]
    for n, row in enumerate(rest):
        gate_ref[chips + n : chips + n + 1] = row
    for i in range(1, chunks):
        gate_ref[chips + 7 + i : chips + 8 + i] = one_if(inner[i : i + 1] == inner[0:1])
    for i in range(2, chunks + 1):
        gate_ref[chips + 9 + i : chips + 10 + i] = one_if(inner[i : i + 1] == inner[1:2])

    @pl.loop(0, pairs)
    def _(p):
        finish_all(fetch(p))
        for n in (0, 1):
            cols = slice(n * HEAD, (n + 1) * HEAD)
            ext_k[n, CHUNK - 8 :] = kb[p, :, cols].astype(F32)
            ext_v[n, CHUNK - 8 :] = vb[p, :, cols].astype(F32)
        taps = [(0.5 * w_ref[1, :, lanes(2 * p + n)], w_ref[2, :, lanes(2 * p + n)]) for n in (0, 1)]
        states = [jnp.zeros((HEAD, HEAD), F32)] * 2
        for i in range(1, chunks):
            r0 = i * CHUNK
            same = one_if(doc_s[8 + r0 - 1 : 8 + r0] == doc_s[8 + r0 + CHUNK - 1 : 8 + r0 + CHUNK])
            for n in (0, 1):
                key, val, tail = kv_chunk(ext_k.at[n], ext_v.at[n], *taps[n], m_s, live_s, r0)
                pkb[2 * p + n, r0 - CHUNK : r0] = key
                valb[2 * p + n, r0 - CHUNK : r0] = val
                states[n] = states[n] * same + tail
                st_ref[2 * p + n, i - 1] = states[n]
        run(store(p))

    finish_all(edges)
    for p in range(pairs):
        finish_all(store(p))


def first_kernel(
    here_ref, len_ref, gate_ref, k_ref, v_ref, rim_ref, w_ref, late_ref,
    pk_ref, val_ref, st_ref, tail_ref, doc_s, m_s, live_s, ext_k, ext_v,
    *, mine, rows, chips,
):
    heads = pk_ref.shape[0]
    here = here_ref[0]
    base = (here % 2 if mine else 1 - here % 2) * heads
    count = late_ref.shape[1] + 1
    fill_doc(here * rows, starts_of(len_ref[...]), doc_s, m_s)
    fill_live(doc_s, live_s)

    @pl.loop(0, heads // 2)
    def _(p):
        for n in (0, 1):
            cols = lanes(base + 2 * p + n)
            ext_k[n, 0:8] = rim_ref[1, :, cols].astype(F32)
            ext_v[n, 0:8] = rim_ref[2, :, cols].astype(F32)
            ext_k[n, 8:] = k_ref[:, cols].astype(F32)
            ext_v[n, 8:] = v_ref[:, cols].astype(F32)
        for n in (0, 1):
            h = 2 * p + n
            cols = lanes(base + h)
            key, val, tail = kv_chunk(
                ext_k.at[n], ext_v.at[n], 0.5 * w_ref[1, :, cols], w_ref[2, :, cols], m_s, live_s, 0
            )
            pk_ref[h] = key
            val_ref[h] = val
            st_ref[h, 0] = tail.astype(BF16)
            for i in range(1, count):
                state = late_ref[base + h, i - 1] + tail * gate_ref[chips + 10 + i : chips + 11 + i]
                if i < count - 1:
                    st_ref[h, i] = state.astype(BF16)
            tail_ref[h] = state.astype(BF16)


def attend_kernel(
    here_ref, len_ref, q_hbm, pkl_hbm, vall_hbm, pkf_ref, valf_ref, rim_ref, w_ref,
    pq_out, mix_out, doc_s, m_s, use_s, ext, allow_s, qb, kb, vb, in_sem, *staging,
    mine,
):
    heads, rows, _ = pq_out.shape
    chunks = rows // CHUNK
    pairs = heads // 2
    here = here_ref[0]
    base = (here % 2 if mine else 1 - here % 2) * heads
    if mine:
        kf_s, vf_s, first_sem = staging
        firsts = [
            pltpu.make_async_copy(pkf_ref, kf_s, first_sem.at[0]),
            pltpu.make_async_copy(valf_ref, vf_s, first_sem.at[1]),
        ]
        pq_ref, mix_ref, pkf_ref, valf_ref = pq_out, mix_out, kf_s, vf_s
    else:
        firsts = []
        pq_ref, mix_ref, out_sem = staging

    def fetch(p):
        two = pl.ds(base + 2 * p, 2)
        return [
            pltpu.make_async_copy(q_hbm.at[:, lanes(base + 2 * p, 2)], qb.at[p], in_sem.at[0, p]),
            pltpu.make_async_copy(pkl_hbm.at[two], kb.at[p], in_sem.at[1, p]),
            pltpu.make_async_copy(vall_hbm.at[two], vb.at[p], in_sem.at[2, p]),
        ]

    def store(p):
        two = pl.ds(2 * p, 2)
        return [
            pltpu.make_async_copy(pq_ref.at[two], pq_out.at[two], out_sem.at[0, p]),
            pltpu.make_async_copy(mix_ref.at[two], mix_out.at[two], out_sem.at[1, p]),
        ]

    run(firsts)
    for p in range(pairs):
        run(fetch(p))

    below = fill_doc(here * rows, starts_of(len_ref[...]), doc_s, m_s)
    across = lax.dot_general(
        jnp.ones((8, HEAD), BF16), below[8:], (((1,), (1,)), ((), ())), preferred_element_type=F32
    )
    causal = lax.broadcasted_iota(jnp.int32, (CHUNK, CHUNK), 1) <= lax.broadcasted_iota(
        jnp.int32, (CHUNK, CHUNK), 0
    )
    for i in range(chunks):
        r0 = i * CHUNK
        doc = doc_s[8 + r0 : 8 + r0 + CHUNK]
        same = wide(doc) == across[0:1, r0 : r0 + CHUNK]
        allow_s[i] = jnp.where(same & causal, 1.0, 0.0).astype(BF16)
        use_s[r0 : r0 + CHUNK] = one_if(doc == doc_s[8 + r0 - 1 : 8 + r0]).astype(BF16)
    finish_all(firsts)

    @pl.loop(0, pairs)
    def _(p):
        finish_all(fetch(p))
        for n in (0, 1):
            ext[n, 0:8] = rim_ref[0, :, lanes(base + 2 * p + n)].astype(F32)
            ext[n, 8:] = qb[p, :, n * HEAD : (n + 1) * HEAD].astype(F32)
        taps = [0.5 * w_ref[0, :, lanes(base + 2 * p + n)] for n in (0, 1)]

        def make(i, n):
            rows = slice(i * CHUNK, (i + 1) * CHUNK)
            query = silu_of_half(conv(ext.at[n], taps[n], m_s, i * CHUNK)).astype(BF16)
            pq_ref[2 * p + n, rows] = query * use_s[rows]
            return query

        def mixed(i, n, query):
            r0 = i * CHUNK
            key = pkf_ref[2 * p + n] if i == 0 else kb[p, n, r0 - CHUNK : r0]
            val = valf_ref[2 * p + n] if i == 0 else vb[p, n, r0 - CHUNK : r0]
            scores = lax.dot_general(query, key, (((1,), (1,)), ((), ())), preferred_element_type=F32)
            weights = scores.astype(BF16) * allow_s[i]
            mix = jnp.dot(weights, val, preferred_element_type=F32)
            mix_ref[2 * p + n, r0 : r0 + CHUNK] = mix.astype(BF16)

        ahead = None
        for i in range(chunks):
            for n in (0, 1):
                query = make(i, n)
                if ahead is not None:
                    mixed(*ahead)
                ahead = (i, n, query)
        mixed(*ahead)
        if not mine:
            run(store(p))

    if not mine:
        for p in range(pairs):
            finish_all(store(p))


def finish_kernel(here_ref, gate_ref, pq_ref, mix_ref, st_ref, carried_ref, gain_ref, *rest, mine, chips):
    if mine:
        pqx_hbm, mixx_hbm, out_hbm, pqx_ref, mixx_ref, outb, out_sem, next_sem = rest
        onward = [
            pltpu.make_async_copy(pqx_hbm, pqx_ref, next_sem.at[0]),
            pltpu.make_async_copy(mixx_hbm, mixx_ref, next_sem.at[1]),
        ]
    else:
        _, out_hbm, outb, out_sem = rest
        onward = []
    heads, rows, _ = pq_ref.shape
    chunks = rows // CHUNK
    base = (here_ref[0] % 2 if mine else 1 - here_ref[0] % 2) * heads
    mean = jnp.full((HEAD, HEAD), 1.0 / HEAD, BF16)
    run(onward)

    def store(p, i):
        rows = pl.ds(i * CHUNK, CHUNK)
        return pltpu.make_async_copy(
            outb.at[p, rows], out_hbm.at[rows, lanes(base + 2 * p, 2)], out_sem.at[p, i]
        )

    @pl.loop(0, heads // 2)
    def _(p):
        gain = [gain_ref[:, lanes(base + 2 * p + n)] for n in (0, 1)]

        def blend(i, n):
            h = 2 * p + n
            state = carried_ref[h].astype(F32)
            if i:
                state = st_ref[h, i - 1].astype(F32) + state * gate_ref[chips + 7 + i : chips + 8 + i]
            rows = slice(i * CHUNK, (i + 1) * CHUNK)
            held = jnp.dot(pq_ref[h, rows], state.astype(BF16), preferred_element_type=F32)
            return mix_ref[h, rows].astype(F32) + held

        def norm(i, n, mixture):
            square = jnp.dot((mixture * mixture).astype(BF16), mean, preferred_element_type=F32)
            scale = lax.rsqrt(square + 1e-06) * gain[n]
            outb[p, i * CHUNK : (i + 1) * CHUNK, n * HEAD : (n + 1) * HEAD] = (mixture * scale).astype(BF16)
            if n:
                store(p, i).start()

        ahead = None
        for i in range(chunks):
            for n in (0, 1):
                mixture = blend(i, n)
                if ahead is not None:
                    norm(*ahead)
                ahead = (i, n, mixture)
        norm(*ahead)

    finish_all(onward)
    for p in range(heads // 2):
        for i in range(chunks):
            store(p, i).wait()


def rim_kernel(q_ref, k_ref, v_ref, out_ref):
    out_ref[0] = q_ref[...]
    out_ref[1] = k_ref[...]
    out_ref[2] = v_ref[...]


def join_kernel(gate_ref, own_ref, got_ref, out_ref, *, chips):
    own, got = gate_ref[chips : chips + 1], gate_ref[chips + 1 : chips + 2]
    out_ref[...] = (own_ref[...].astype(F32) * own + got_ref[...].astype(F32) * got).astype(BF16)


def enter_kernel(gate_ref, spread_ref, out_ref):
    running = jnp.zeros(spread_ref.shape[1:], F32)
    for n in range(spread_ref.shape[0]):
        out_ref[n] = running.astype(BF16)
        running = running * gate_ref[n : n + 1] + spread_ref[n].astype(F32)


def carry_kernel(gate_ref, entered_ref, own_ref, got_ref, mine_ref, other_ref, *, chips):
    gate = [gate_ref[chips + 2 + n : chips + 3 + n] for n in range(4)]
    entered = entered_ref[...].astype(F32)
    mine_ref[...] = (entered * gate[0] + got_ref[...].astype(F32) * gate[1]).astype(BF16)
    other_ref[...] = (entered * gate[2] + own_ref[...].astype(F32) * gate[3]).astype(BF16)


def in_hbm(x):
    return pltpu.with_memory_space_constraint(x, pltpu.HBM)


def params(mib):
    return pltpu.CompilerParams(vmem_limit_bytes=mib * 1024 * 1024)


def small(kernel, outs, *args):
    return pl.pallas_call(
        kernel, out_shape=outs, compiler_params=pltpu.CompilerParams(vmem_limit_bytes=4 * 1024 * 1024)
    )(*args)


def shaped(*shape, dtype=BF16):
    return jax.ShapeDtypeStruct(shape, dtype)


def per_device(query_rows, key_rows, value_rows, lengths, conv_weight, out_gain):
    query_rows, key_rows, value_rows = (in_hbm(x) for x in (query_rows, key_rows, value_rows))
    rows, channels = query_rows.shape
    heads = channels // HEAD
    half = heads // 2
    chunks = rows // CHUNK
    chips = lax.axis_size("x") * lax.axis_size("z")
    ctx_count = 2 * chips
    here = lax.axis_index(CTX).astype(jnp.int32).reshape(1)
    swap = [(0, 1), (1, 0)]

    smem = pl.BlockSpec(memory_space=pltpu.SMEM)
    last_rows = pl.BlockSpec((8, channels), lambda i: (rows // 8 - 1, 0))
    rims = pl.pallas_call(
        rim_kernel,
        grid=(1,),
        in_specs=[last_rows] * 3,
        out_specs=pl.BlockSpec((3, 8, channels), lambda i: (0, 0, 0)),
        out_shape=shaped(3, 8, channels),
        compiler_params=params(4),
        name="rim",
    )(query_rows, key_rows, value_rows)
    rims = lax.ppermute(rims, CTX, [(i, (i + 1) % ctx_count) for i in range(ctx_count)])

    vmem = pl.BlockSpec(memory_space=pltpu.VMEM)
    hbm = pl.BlockSpec(memory_space=pl.ANY)
    lengths = lengths.reshape(1, -1)
    gains = out_gain.reshape(1, -1)
    gate_rows = chips + 16
    pairs, half_pairs = heads // 2, half // 2
    later = rows - CHUNK
    dma = lambda *shape: pltpu.SemaphoreType.DMA(shape)

    def masks(count):
        return [
            pltpu.VMEM((count + 8, HEAD), F32),
            pltpu.VMEM((3, count, HEAD), F32),
            pltpu.VMEM((count, HEAD), BF16),
        ]

    pk_late, val_late, st_late, gates, key_head, value_head = pl.pallas_call(
        lambda *refs: late_kernel(*refs, chips=chips),
        in_specs=[smem, vmem, hbm, hbm, vmem],
        out_specs=[hbm, hbm, vmem, vmem, vmem, vmem],
        out_shape=[
            pltpu.HBM((heads, later, HEAD), BF16),
            pltpu.HBM((heads, later, HEAD), BF16),
            shaped(heads, chunks - 1, HEAD, HEAD, dtype=F32),
            shaped(gate_rows, HEAD, dtype=F32),
            shaped(CHUNK, channels),
            shaped(CHUNK, channels),
        ],
        scratch_shapes=masks(rows)
        + [pltpu.VMEM((2, rows + 8, HEAD), F32)] * 2
        + [pltpu.VMEM((pairs, later + GROUP, 2 * HEAD), BF16)] * 2
        + [pltpu.VMEM((heads, later, HEAD), BF16)] * 2
        + [dma(2, pairs), dma(2, pairs), dma(2)],
        compiler_params=params(20),
        name="late",
    )(here, lengths, key_rows, value_rows, conv_weight)
    pk_late, val_late = in_hbm(pk_late), in_hbm(val_late)

    def first(mine):
        return pl.pallas_call(
            lambda *refs: first_kernel(*refs, mine=mine, rows=rows, chips=chips),
            in_specs=[smem] + [vmem] * 7,
            out_specs=[vmem] * 4,
            out_shape=[
                shaped(half, CHUNK, HEAD),
                shaped(half, CHUNK, HEAD),
                shaped(half, chunks - 1, HEAD, HEAD),
                shaped(half, HEAD, HEAD),
            ],
            scratch_shapes=masks(CHUNK) + [pltpu.VMEM((2, CHUNK + 8, HEAD), F32)] * 2,
            compiler_params=params(8),
            name="first",
        )(here, lengths, gates, key_head, value_head, rims, conv_weight, st_late)

    pk_other, val_other, inner_other, other = first(False)
    got = lax.ppermute(other, "c", swap)
    pk_own, val_own, inner_own, own = first(True)

    state = (half, HEAD, HEAD)
    chip_tail = small(lambda *r: join_kernel(*r, chips=chips), shaped(*state), gates, own, got)
    spread = lax.all_to_all(chip_tail.reshape(chips, -1, HEAD), ("x", "z"), 0, 0, tiled=True)

    def attend(mine, pk_first, val_first):
        shape = (half, rows, HEAD)
        return pl.pallas_call(
            lambda *refs: attend_kernel(*refs, mine=mine),
            in_specs=[smem, vmem, hbm, hbm, hbm] + [hbm if mine else vmem] * 2 + [vmem, vmem],
            out_specs=[vmem if mine else hbm] * 2,
            out_shape=[shaped(*shape) if mine else pltpu.HBM(shape, BF16)] * 2,
            scratch_shapes=masks(rows)
            + [pltpu.VMEM((2, rows + 8, HEAD), F32), pltpu.VMEM((chunks, CHUNK, CHUNK), BF16)]
            + [pltpu.VMEM((half_pairs, rows, 2 * HEAD), BF16)]
            + [pltpu.VMEM((half_pairs, 2, later, HEAD), BF16)] * 2
            + [dma(3, half_pairs)]
            + (
                [pltpu.VMEM((half, CHUNK, HEAD), BF16)] * 2 + [dma(2)]
                if mine
                else [pltpu.VMEM(shape, BF16)] * 2 + [dma(2, half_pairs)]
            ),
            compiler_params=params(24),
            name="attend",
        )(here, lengths, query_rows, pk_late, val_late, pk_first, val_first, rims, conv_weight)

    phi_other, mix_other = (in_hbm(x) for x in attend(False, pk_other, val_other))
    phi_own, mix_own = attend(True, in_hbm(pk_own), in_hbm(val_own))

    entering = small(enter_kernel, shaped(*spread.shape), gates, spread)
    entered = lax.all_to_all(entering, ("x", "z"), 0, 0, tiled=True).reshape(state)
    carried_own, carried_other = small(
        lambda *r: carry_kernel(*r, chips=chips), [shaped(*state)] * 2, gates, entered, own, got
    )
    carried_far = lax.ppermute(carried_other, "c", swap)

    def finish(mine, phi, mix, inner, carried, *others):
        shape = (half, rows, HEAD)
        ahead = [shaped(*shape)] * 2 if mine else []
        args = (here, gates, phi, mix, inner, carried, gains, *others)
        return pl.pallas_call(
            lambda *refs: finish_kernel(*refs, mine=mine, chips=chips),
            in_specs=[smem] + [vmem] * 6 + [hbm] * len(others),
            out_specs=[hbm] + [vmem] * len(ahead),
            out_shape=[pltpu.HBM((rows, channels), BF16)] + ahead,
            scratch_shapes=[pltpu.VMEM((half_pairs, rows, 2 * HEAD), BF16), dma(half_pairs, chunks)]
            + ([dma(2)] if mine else []),
            input_output_aliases={} if mine else {len(args) - 1: 0},
            compiler_params=params(12),
            name="finish",
        )(*args)

    done, phi_other, mix_other = finish(
        True, phi_own, mix_own, inner_own, carried_own, phi_other, mix_other
    )
    return finish(False, phi_other, mix_other, inner_other, carried_far, done)[0]


def solution(mesh):
    finer = Mesh(mesh.devices.reshape(mesh.shape["dp"], 4, 8, 2), DP_CTX)

    return jax.shard_map(
        per_device,
        mesh=finer,
        in_specs=(P(DP_CTX, None), P(DP_CTX, None), P(DP_CTX, None), P("dp"), P(), P()),
        out_specs=P(DP_CTX, None),
        check_vma=False,
    )
```

```python
import jax
import jax.numpy as jnp
from jax import lax
from jax.experimental import pallas as pl
from jax.experimental.pallas import tpu as pltpu
from jax.sharding import Mesh
from jax.sharding import PartitionSpec as P

HEAD = 128
CHUNK = 256
GROUP = 16
BLOCK = 256
CTX = ("x", "z", "c")
DP_CTX = ("dp", "x", "z", "c")
F32 = jnp.float32
BF16 = jnp.bfloat16


def one_if(flag):
    return jnp.where(flag, 1.0, 0.0)


def starts_of(lengths):
    rows = jnp.broadcast_to(lengths, (8, HEAD))
    before = one_if(
        lax.broadcasted_iota(jnp.int32, (HEAD, HEAD), 0) < lax.broadcasted_iota(jnp.int32, (HEAD, HEAD), 1)
    ).astype(BF16)
    high = jnp.dot((rows >> 8).astype(F32).astype(BF16), before, preferred_element_type=F32)
    low = jnp.dot((rows & 255).astype(F32).astype(BF16), before, preferred_element_type=F32)
    return high * 256.0 + low


def docs_of(positions, starts):
    below = one_if(starts[0:1] <= positions.astype(F32)).astype(BF16)
    return jnp.dot(below, jnp.ones((HEAD, HEAD), BF16), preferred_element_type=F32), below


def wide(rows):
    return jnp.concatenate([rows, rows], axis=1)


def fill_doc(first, starts, doc_s, m_s):
    count = m_s.shape[1]
    iota = lax.broadcasted_iota(jnp.int32, (count + 8, HEAD), 0)
    doc, below = docs_of(iota + (first - 8), starts)
    doc_s[...] = doc
    for j in (1, 2, 3):
        m_s[j - 1] = one_if(doc_s[8 - j : 8 - j + count] == doc_s[8:])
    return below


def conv(ext, taps, m_s, r0):
    acc = taps[0:1] * ext[8 + r0 : 8 + r0 + CHUNK]
    for j in (1, 2, 3):
        acc += taps[j : j + 1] * (ext[8 + r0 - j : 8 + r0 - j + CHUNK] * m_s[j - 1, r0 : r0 + CHUNK])
    return acc


def silu_of_half(half):
    return half * jnp.tanh(half) + half


def fill_live(doc, live_s):
    for r0 in range(0, live_s.shape[0], CHUNK):
        last = doc[8 + r0 + CHUNK - 1 : 8 + r0 + CHUNK]
        live_s[r0 : r0 + CHUNK] = one_if(doc[8 + r0 : 8 + r0 + CHUNK] == last).astype(BF16)


def kv_chunk(ext_k, ext_v, kw, vw, m_s, live_s, r0):
    key = silu_of_half(conv(ext_k, kw, m_s, r0)).astype(BF16)
    val = conv(ext_v, vw, m_s, r0).astype(BF16)
    live = live_s[r0 : r0 + CHUNK]
    tail = lax.dot_general(key * live, val, (((0,), (0,)), ((), ())), preferred_element_type=F32)
    return key, val, tail


def lanes(head, count=1):
    return pl.ds(pl.multiple_of(head * HEAD, HEAD), count * HEAD)


def run(copies):
    for copy in copies:
        copy.start()


def finish_all(copies):
    for copy in copies:
        copy.wait()


def late_kernel(
    here_ref, len_ref, k_hbm, v_hbm, w_ref,
    pk_hbm, val_hbm, st_ref, gate_ref, k0_ref, v0_ref, m0_ref, live0_ref,
    doc_s, m_s, live_s, ext_k, ext_v, kb, vb, pkb, valb, in_sem, out_sem, edge_sem,
    *, chips,
):
    rows = k_hbm.shape[0]
    chunks = rows // CHUNK
    pairs = kb.shape[0]
    tail_rows = pl.ds(CHUNK - GROUP, rows - CHUNK + GROUP)

    def head_of(p):
        return 2 * ((p + (1 - here_ref[0] % 2) * (pairs // 2)) % pairs)

    def fetch(p):
        cols = lanes(head_of(p), 2)
        return [
            pltpu.make_async_copy(k_hbm.at[tail_rows, cols], kb.at[p], in_sem.at[0, p]),
            pltpu.make_async_copy(v_hbm.at[tail_rows, cols], vb.at[p], in_sem.at[1, p]),
        ]

    def store(p):
        two = pl.ds(2 * p, 2)
        return [
            pltpu.make_async_copy(pkb.at[two], pk_hbm.at[two], out_sem.at[0, p]),
            pltpu.make_async_copy(valb.at[two], val_hbm.at[two], out_sem.at[1, p]),
        ]

    edges = [
        pltpu.make_async_copy(k_hbm.at[pl.ds(0, CHUNK)], k0_ref, edge_sem.at[0]),
        pltpu.make_async_copy(v_hbm.at[pl.ds(0, CHUNK)], v0_ref, edge_sem.at[1]),
    ]
    for p in range(pairs):
        run(fetch(p))
    run(edges)

    here = here_ref[0]
    core = here % 2
    offset = here * rows
    starts = starts_of(len_ref[...])
    fill_doc(offset, starts, doc_s, m_s)
    fill_live(doc_s, live_s)
    m0_ref[...] = m_s[:, :CHUNK]
    live0_ref[...] = live_s[:CHUNK]
    chip = offset - core * rows
    chip_mark = lax.broadcasted_iota(jnp.int32, (chips + 8, HEAD), 0)
    mark = lax.broadcasted_iota(jnp.int32, (16, HEAD), 0)
    ends, _ = docs_of(chip_mark * (2 * rows) - 1, starts)
    mine, _ = docs_of(chip + mark * rows - 1, starts)
    inner, _ = docs_of(offset + mark * CHUNK - 1, starts)
    keep_first = one_if(mine[1:2] == mine[0:1])
    keep_second = one_if(mine[2:3] == mine[1:2])
    second = jnp.full((1, HEAD), core, jnp.int32) == 1
    gate_ref[0:chips] = one_if(ends[1 : chips + 1] == ends[0:chips])
    one, zero = jnp.ones((1, HEAD), F32), jnp.zeros((1, HEAD), F32)
    rest = [
        jnp.where(second, one, keep_second),
        jnp.where(second, keep_second, one),
        jnp.where(second, keep_first, one),
        jnp.where(second, one, zero),
        jnp.where(second, one, keep_first),
        jnp.where(second, zero, one),
    ]
    for n, row in enumerate(rest):
        gate_ref[chips + n : chips + n + 1] = row
    for i in range(1, chunks):
        gate_ref[chips + 7 + i : chips + 8 + i] = one_if(inner[i : i + 1] == inner[0:1])
    for i in range(2, chunks + 1):
        gate_ref[chips + 9 + i : chips + 10 + i] = one_if(inner[i : i + 1] == inner[1:2])

    @pl.loop(0, pairs)
    def _(p):
        finish_all(fetch(p))
        for n in (0, 1):
            cols = slice(n * HEAD, (n + 1) * HEAD)
            ext_k[n, CHUNK - 8 :] = kb[p, :, cols].astype(F32)
            ext_v[n, CHUNK - 8 :] = vb[p, :, cols].astype(F32)
        head = head_of(p)
        taps = [(0.5 * w_ref[1, :, lanes(head + n)], w_ref[2, :, lanes(head + n)]) for n in (0, 1)]
        states = [jnp.zeros((HEAD, HEAD), F32)] * 2
        for i in range(1, chunks):
            r0 = i * CHUNK
            same = one_if(doc_s[8 + r0 - 1 : 8 + r0] == doc_s[8 + r0 + CHUNK - 1 : 8 + r0 + CHUNK])
            for n in (0, 1):
                key, val, tail = kv_chunk(ext_k.at[n], ext_v.at[n], *taps[n], m_s, live_s, r0)
                pkb[2 * p + n, r0 - CHUNK : r0] = key
                valb[2 * p + n, r0 - CHUNK : r0] = val
                states[n] = states[n] * same + tail
                st_ref[head + n, i - 1] = states[n]

        @pl.when(p < pairs // 2)
        def _():
            run(store(p))

    finish_all(edges)
    for p in range(pairs // 2):
        finish_all(store(p))


def first_kernel(
    here_ref, gate_ref, k_ref, v_ref, m_ref, live_ref, rim_ref, w_ref, late_ref,
    st_ref, tail_ref, ext_k, ext_v,
    *, mine, chips,
):
    heads = tail_ref.shape[0]
    here = here_ref[0]
    base = (here % 2 if mine else 1 - here % 2) * heads
    count = late_ref.shape[1] + 1

    @pl.loop(0, heads // 2)
    def _(p):
        for n in (0, 1):
            cols = lanes(base + 2 * p + n)
            ext_k[n, 0:8] = rim_ref[1, :, cols].astype(F32)
            ext_v[n, 0:8] = rim_ref[2, :, cols].astype(F32)
            ext_k[n, 8:] = k_ref[:, cols].astype(F32)
            ext_v[n, 8:] = v_ref[:, cols].astype(F32)
        for n in (0, 1):
            h = 2 * p + n
            cols = lanes(base + h)
            _, _, tail = kv_chunk(
                ext_k.at[n], ext_v.at[n], 0.5 * w_ref[1, :, cols], w_ref[2, :, cols], m_ref, live_ref, 0
            )
            st_ref[h, 0] = tail.astype(BF16)
            for i in range(1, count):
                state = late_ref[base + h, i - 1] + tail * gate_ref[chips + 10 + i : chips + 11 + i]
                if i < count - 1:
                    st_ref[h, i] = state.astype(BF16)
            tail_ref[h] = state.astype(BF16)


def attend_kernel(
    here_ref, len_ref, q_hbm, k_hbm, v_hbm, rim_ref, w_ref, *rest, mine,
):
    if mine:
        pq_ref, mix_ref, doc_s, m_s, use_s, ext, ext_k, ext_v, allow_s, qb, k0b, v0b, in_sem = rest
    else:
        (pk_hbm, val_hbm, pq_out, mix_out, doc_s, m_s, use_s, ext, ext_k, ext_v, allow_s,
         qb, k0b, v0b, in_sem, kb, vb, pq_ref, mix_ref, late_sem, out_sem) = rest
    pairs, rows, _ = pq_ref.shape
    chunks = rows // CHUNK
    here = here_ref[0]
    base = (here % 2 if mine else 1 - here % 2) * 2 * pairs
    made = pl.ds(0, k0b.shape[1])

    def fetch(p):
        cols, two = lanes(base + 2 * p, 2), pl.ds(2 * p, 2)
        copies = [
            pltpu.make_async_copy(q_hbm.at[:, cols], qb.at[p], in_sem.at[0, p]),
            pltpu.make_async_copy(k_hbm.at[made, cols], k0b.at[p], in_sem.at[1, p]),
            pltpu.make_async_copy(v_hbm.at[made, cols], v0b.at[p], in_sem.at[2, p]),
        ]
        if not mine:
            copies += [
                pltpu.make_async_copy(pk_hbm.at[two], kb.at[p], late_sem.at[0, p]),
                pltpu.make_async_copy(val_hbm.at[two], vb.at[p], late_sem.at[1, p]),
            ]
        return copies

    def store(p):
        return [
            pltpu.make_async_copy(pq_ref.at[p], pq_out.at[p], out_sem.at[0, p]),
            pltpu.make_async_copy(mix_ref.at[p], mix_out.at[p], out_sem.at[1, p]),
        ]

    for p in range(pairs):
        run(fetch(p))

    below = fill_doc(here * rows, starts_of(len_ref[...]), doc_s, m_s)
    across = lax.dot_general(
        jnp.ones((8, HEAD), BF16), below[8:], (((1,), (1,)), ((), ())), preferred_element_type=F32
    )
    causal = lax.broadcasted_iota(jnp.int32, (CHUNK, CHUNK), 1) <= lax.broadcasted_iota(
        jnp.int32, (CHUNK, CHUNK), 0
    )
    for i in range(chunks):
        r0 = i * CHUNK
        doc = doc_s[8 + r0 : 8 + r0 + CHUNK]
        same = wide(doc) == across[0:1, r0 : r0 + CHUNK]
        allow_s[i] = jnp.where(same & causal, 1.0, 0.0).astype(BF16)
        use_s[r0 : r0 + CHUNK] = one_if(doc == doc_s[8 + r0 - 1 : 8 + r0]).astype(BF16)

    @pl.loop(0, pairs)
    def _(p):
        finish_all(fetch(p))
        taps = []
        for n in (0, 1):
            cols, head = slice(n * HEAD, (n + 1) * HEAD), lanes(base + 2 * p + n)
            for which, buffer, rows in ((0, ext, qb), (1, ext_k, k0b), (2, ext_v, v0b)):
                buffer[n, 0:8] = rim_ref[which, :, head].astype(F32)
                buffer[n, 8:] = rows[p, :, cols].astype(F32)
            taps.append((0.5 * w_ref[0, :, head], 0.5 * w_ref[1, :, head], w_ref[2, :, head]))

        def make(i, n):
            r0 = i * CHUNK
            rows = slice(r0, r0 + CHUNK)
            query = silu_of_half(conv(ext.at[n], taps[n][0], m_s, r0)).astype(BF16)
            pq_ref[p, rows, n * HEAD : (n + 1) * HEAD] = query * use_s[rows]
            if mine or i == 0:
                key = silu_of_half(conv(ext_k.at[n], taps[n][1], m_s, r0)).astype(BF16)
                val = conv(ext_v.at[n], taps[n][2], m_s, r0).astype(BF16)
            else:
                key, val = kb[p, n, r0 - CHUNK : r0], vb[p, n, r0 - CHUNK : r0]
            return query, key, val

        def mixed(i, n, query, key, val):
            scores = lax.dot_general(query, key, (((1,), (1,)), ((), ())), preferred_element_type=F32)
            weights = scores.astype(BF16) * allow_s[i]
            mix = jnp.dot(weights, val, preferred_element_type=F32)
            mix_ref[p, i * CHUNK : (i + 1) * CHUNK, n * HEAD : (n + 1) * HEAD] = mix.astype(BF16)

        ahead = None
        for i in range(chunks):
            for n in (0, 1):
                made_now = make(i, n)
                if ahead is not None:
                    mixed(*ahead)
                ahead = (i, n) + made_now
        mixed(*ahead)
        if not mine:
            run(store(p))

    if not mine:
        for p in range(pairs):
            finish_all(store(p))


def both(first, second):
    none = jnp.zeros_like(first)
    return jnp.concatenate(
        [jnp.concatenate([first, none], axis=1), jnp.concatenate([none, second], axis=1)], axis=0
    )


def finish_kernel(here_ref, gate_ref, pq_ref, mix_ref, st_ref, carried_ref, gain_ref, *rest, mine, chips):
    if mine:
        pqx_hbm, mixx_hbm, out_hbm, pqx_ref, mixx_ref, outb, out_sem, next_sem = rest
        onward = [
            pltpu.make_async_copy(pqx_hbm, pqx_ref, next_sem.at[0]),
            pltpu.make_async_copy(mixx_hbm, mixx_ref, next_sem.at[1]),
        ]
    else:
        _, out_hbm, outb, out_sem = rest
        onward = []
    pairs, rows, _ = pq_ref.shape
    chunks = rows // CHUNK
    base = (here_ref[0] % 2 if mine else 1 - here_ref[0] % 2) * 2 * pairs
    mean = both(jnp.full((HEAD, HEAD), 1.0 / HEAD, BF16), jnp.full((HEAD, HEAD), 1.0 / HEAD, BF16))
    run(onward)

    def store(p, i):
        rows = pl.ds(i * CHUNK, CHUNK)
        return pltpu.make_async_copy(
            outb.at[p, rows], out_hbm.at[rows, lanes(base + 2 * p, 2)], out_sem.at[p, i]
        )

    @pl.loop(0, pairs)
    def _(p):
        gain = gain_ref[:, lanes(base + 2 * p, 2)]

        def entering(h, i):
            if not i:
                return carried_ref[h]
            kept = carried_ref[h].astype(F32) * gate_ref[chips + 7 + i : chips + 8 + i]
            return (st_ref[h, i - 1].astype(F32) + kept).astype(BF16)

        def blend(at, state):
            held = jnp.dot(pq_ref[p, at : at + BLOCK], state, preferred_element_type=F32)
            return mix_ref[p, at : at + BLOCK].astype(F32) + held

        def norm(at, mixture):
            square = jnp.dot((mixture * mixture).astype(BF16), mean, preferred_element_type=F32)
            scale = lax.rsqrt(square + 1e-06) * gain
            outb[p, at : at + BLOCK] = (mixture * scale).astype(BF16)
            if (at + BLOCK) % CHUNK == 0:
                store(p, at // CHUNK).start()

        ahead = None
        for i in range(chunks):
            state = both(entering(2 * p, i), entering(2 * p + 1, i))
            for at in range(i * CHUNK, (i + 1) * CHUNK, BLOCK):
                mixture = blend(at, state)
                if ahead is not None:
                    norm(*ahead)
                ahead = (at, mixture)
        norm(*ahead)

    finish_all(onward)
    for p in range(pairs):
        for i in range(chunks):
            store(p, i).wait()


def rim_kernel(q_ref, k_ref, v_ref, out_ref):
    out_ref[0] = q_ref[...]
    out_ref[1] = k_ref[...]
    out_ref[2] = v_ref[...]


def join_kernel(gate_ref, own_ref, got_ref, out_ref, *, chips):
    own, got = gate_ref[chips : chips + 1], gate_ref[chips + 1 : chips + 2]
    out_ref[...] = (own_ref[...].astype(F32) * own + got_ref[...].astype(F32) * got).astype(BF16)


def enter_kernel(gate_ref, spread_ref, out_ref):
    running = jnp.zeros(spread_ref.shape[1:], F32)
    for n in range(spread_ref.shape[0]):
        out_ref[n] = running.astype(BF16)
        running = running * gate_ref[n : n + 1] + spread_ref[n].astype(F32)


def carry_kernel(gate_ref, entered_ref, own_ref, got_ref, mine_ref, other_ref, *, chips):
    gate = [gate_ref[chips + 2 + n : chips + 3 + n] for n in range(4)]
    entered = entered_ref[...].astype(F32)
    mine_ref[...] = (entered * gate[0] + got_ref[...].astype(F32) * gate[1]).astype(BF16)
    other_ref[...] = (entered * gate[2] + own_ref[...].astype(F32) * gate[3]).astype(BF16)


def in_hbm(x):
    return pltpu.with_memory_space_constraint(x, pltpu.HBM)


def params(mib):
    return pltpu.CompilerParams(vmem_limit_bytes=mib * 1024 * 1024)


def small(kernel, outs, *args):
    return pl.pallas_call(
        kernel, out_shape=outs, compiler_params=pltpu.CompilerParams(vmem_limit_bytes=4 * 1024 * 1024)
    )(*args)


def shaped(*shape, dtype=BF16):
    return jax.ShapeDtypeStruct(shape, dtype)


def per_device(query_rows, key_rows, value_rows, lengths, conv_weight, out_gain):
    query_rows, key_rows, value_rows = (in_hbm(x) for x in (query_rows, key_rows, value_rows))
    rows, channels = query_rows.shape
    heads = channels // HEAD
    half = heads // 2
    chunks = rows // CHUNK
    chips = lax.axis_size("x") * lax.axis_size("z")
    ctx_count = 2 * chips
    here = lax.axis_index(CTX).astype(jnp.int32).reshape(1)
    swap = [(0, 1), (1, 0)]

    smem = pl.BlockSpec(memory_space=pltpu.SMEM)
    last_rows = pl.BlockSpec((8, channels), lambda i: (rows // 8 - 1, 0))
    rims = pl.pallas_call(
        rim_kernel,
        grid=(1,),
        in_specs=[last_rows] * 3,
        out_specs=pl.BlockSpec((3, 8, channels), lambda i: (0, 0, 0)),
        out_shape=shaped(3, 8, channels),
        compiler_params=params(4),
        name="rim",
    )(query_rows, key_rows, value_rows)
    rims = lax.ppermute(rims, CTX, [(i, (i + 1) % ctx_count) for i in range(ctx_count)])

    vmem = pl.BlockSpec(memory_space=pltpu.VMEM)
    hbm = pl.BlockSpec(memory_space=pl.ANY)
    lengths = lengths.reshape(1, -1)
    gains = out_gain.reshape(1, -1)
    gate_rows = chips + 16
    pairs, half_pairs = heads // 2, half // 2
    later = rows - CHUNK
    dma = lambda *shape: pltpu.SemaphoreType.DMA(shape)

    def masks(count):
        return [
            pltpu.VMEM((count + 8, HEAD), F32),
            pltpu.VMEM((3, count, HEAD), F32),
            pltpu.VMEM((count, HEAD), BF16),
        ]

    pk_late, val_late, st_late, gates, key_head, value_head, inside, live = pl.pallas_call(
        lambda *refs: late_kernel(*refs, chips=chips),
        in_specs=[smem, vmem, hbm, hbm, vmem],
        out_specs=[hbm, hbm] + [vmem] * 6,
        out_shape=[
            pltpu.HBM((half, later, HEAD), BF16),
            pltpu.HBM((half, later, HEAD), BF16),
            shaped(heads, chunks - 1, HEAD, HEAD, dtype=F32),
            shaped(gate_rows, HEAD, dtype=F32),
            shaped(CHUNK, channels),
            shaped(CHUNK, channels),
            shaped(3, CHUNK, HEAD, dtype=F32),
            shaped(CHUNK, HEAD),
        ],
        scratch_shapes=masks(rows)
        + [pltpu.VMEM((2, rows + 8, HEAD), F32)] * 2
        + [pltpu.VMEM((pairs, later + GROUP, 2 * HEAD), BF16)] * 2
        + [pltpu.VMEM((heads, later, HEAD), BF16)] * 2
        + [dma(2, pairs), dma(2, half_pairs), dma(2)],
        compiler_params=params(20),
        name="late",
    )(here, lengths, key_rows, value_rows, conv_weight)
    pk_late, val_late = in_hbm(pk_late), in_hbm(val_late)

    def first(mine):
        return pl.pallas_call(
            lambda *refs: first_kernel(*refs, mine=mine, chips=chips),
            in_specs=[smem] + [vmem] * 8,
            out_specs=[vmem] * 2,
            out_shape=[
                shaped(half, chunks - 1, HEAD, HEAD),
                shaped(half, HEAD, HEAD),
            ],
            scratch_shapes=[pltpu.VMEM((2, CHUNK + 8, HEAD), F32)] * 2,
            compiler_params=params(8),
            name="first",
        )(here, gates, key_head, value_head, inside, live, rims, conv_weight, st_late)

    inner_other, other = first(False)
    got = lax.ppermute(other, "c", swap)
    inner_own, own = first(True)

    state = (half, HEAD, HEAD)
    chip_tail = small(lambda *r: join_kernel(*r, chips=chips), shaped(*state), gates, own, got)
    spread = lax.all_to_all(chip_tail.reshape(chips, -1, HEAD), ("x", "z"), 0, 0, tiled=True)

    def attend(mine, *ready):
        shape = (half_pairs, rows, 2 * HEAD)
        made = rows if mine else CHUNK
        return pl.pallas_call(
            lambda *refs: attend_kernel(*refs, mine=mine),
            in_specs=[smem, vmem, hbm, hbm, hbm, vmem, vmem] + [hbm] * len(ready),
            out_specs=[vmem if mine else hbm] * 2,
            out_shape=[shaped(*shape) if mine else pltpu.HBM(shape, BF16)] * 2,
            scratch_shapes=masks(rows)
            + [pltpu.VMEM((2, rows + 8, HEAD), F32)]
            + [pltpu.VMEM((2, made + 8, HEAD), F32)] * 2
            + [pltpu.VMEM((chunks, CHUNK, CHUNK), BF16), pltpu.VMEM(shape, BF16)]
            + [pltpu.VMEM((half_pairs, made, 2 * HEAD), BF16)] * 2
            + [dma(3, half_pairs)]
            + (
                []
                if mine
                else [pltpu.VMEM((half_pairs, 2, later, HEAD), BF16)] * 2
                + [pltpu.VMEM(shape, BF16)] * 2
                + [dma(2, half_pairs)] * 2
            ),
            compiler_params=params(24),
            name="attend",
        )(here, lengths, query_rows, key_rows, value_rows, rims, conv_weight, *ready)

    phi_other, mix_other = (in_hbm(x) for x in attend(False, pk_late, val_late))
    phi_own, mix_own = attend(True)

    entering = small(enter_kernel, shaped(*spread.shape), gates, spread)
    entered = lax.all_to_all(entering, ("x", "z"), 0, 0, tiled=True).reshape(state)
    carried_own, carried_other = small(
        lambda *r: carry_kernel(*r, chips=chips), [shaped(*state)] * 2, gates, entered, own, got
    )
    carried_far = lax.ppermute(carried_other, "c", swap)

    def finish(mine, phi, mix, inner, carried, *others):
        shape = (half_pairs, rows, 2 * HEAD)
        ahead = [shaped(*shape)] * 2 if mine else []
        args = (here, gates, phi, mix, inner, carried, gains, *others)
        return pl.pallas_call(
            lambda *refs: finish_kernel(*refs, mine=mine, chips=chips),
            in_specs=[smem] + [vmem] * 6 + [hbm] * len(others),
            out_specs=[hbm] + [vmem] * len(ahead),
            out_shape=[pltpu.HBM((rows, channels), BF16)] + ahead,
            scratch_shapes=[pltpu.VMEM((half_pairs, rows, 2 * HEAD), BF16), dma(half_pairs, chunks)]
            + ([dma(2)] if mine else []),
            input_output_aliases={} if mine else {len(args) - 1: 0},
            compiler_params=params(12),
            name="finish",
        )(*args)

    done, phi_other, mix_other = finish(
        True, phi_own, mix_own, inner_own, carried_own, phi_other, mix_other
    )
    return finish(False, phi_other, mix_other, inner_other, carried_far, done)[0]


def solution(mesh):
    finer = Mesh(mesh.devices.reshape(mesh.shape["dp"], 4, 8, 2), DP_CTX)

    return jax.shard_map(
        per_device,
        mesh=finer,
        in_specs=(P(DP_CTX, None), P(DP_CTX, None), P(DP_CTX, None), P("dp"), P(), P()),
        out_specs=P(DP_CTX, None),
        check_vma=False,
    )
```

```python
import jax
import jax.numpy as jnp
from jax import lax
from jax.experimental import pallas as pl
from jax.experimental.pallas import tpu as pltpu
from jax.sharding import PartitionSpec as P

HEAD = 128
CHUNK = 256
GROUP = 16
BLOCK = 256
CTX = "ctx"
DP_CTX = ("dp", "ctx")
X_CHIPS = 4
FIRST_X = 3
FIRST_Z = 5
F32 = jnp.float32
BF16 = jnp.bfloat16


def one_if(flag):
    return jnp.where(flag, 1.0, 0.0)


def starts_of(lengths):
    rows = jnp.broadcast_to(lengths, (8, HEAD))
    before = one_if(
        lax.broadcasted_iota(jnp.int32, (HEAD, HEAD), 0) < lax.broadcasted_iota(jnp.int32, (HEAD, HEAD), 1)
    ).astype(BF16)
    high = jnp.dot((rows >> 8).astype(F32).astype(BF16), before, preferred_element_type=F32)
    low = jnp.dot((rows & 255).astype(F32).astype(BF16), before, preferred_element_type=F32)
    return high * 256.0 + low


def docs_of(positions, starts):
    below = one_if(starts[0:1] <= positions.astype(F32)).astype(BF16)
    return jnp.dot(below, jnp.ones((HEAD, HEAD), BF16), preferred_element_type=F32), below


def wide(rows):
    return jnp.concatenate([rows, rows], axis=1)


def fill_doc(first, starts, doc_s, m_s):
    count = m_s.shape[1]
    iota = lax.broadcasted_iota(jnp.int32, (count + 8, HEAD), 0)
    doc, below = docs_of(iota + (first - 8), starts)
    doc_s[...] = doc
    for j in (1, 2, 3):
        m_s[j - 1] = one_if(doc_s[8 - j : 8 - j + count] == doc_s[8:])
    return below


def conv(ext, taps, m_s, r0):
    acc = taps[0:1] * ext[8 + r0 : 8 + r0 + CHUNK]
    for j in (1, 2, 3):
        acc += taps[j : j + 1] * (ext[8 + r0 - j : 8 + r0 - j + CHUNK] * m_s[j - 1, r0 : r0 + CHUNK])
    return acc


def silu_of_half(half):
    return half * jnp.tanh(half) + half


def fill_live(doc, live_s):
    for r0 in range(0, live_s.shape[0], CHUNK):
        last = doc[8 + r0 + CHUNK - 1 : 8 + r0 + CHUNK]
        live_s[r0 : r0 + CHUNK] = one_if(doc[8 + r0 : 8 + r0 + CHUNK] == last).astype(BF16)


def kv_chunk(ext_k, ext_v, kw, vw, m_s, live_s, r0):
    key = silu_of_half(conv(ext_k, kw, m_s, r0)).astype(BF16)
    val = conv(ext_v, vw, m_s, r0).astype(BF16)
    live = live_s[r0 : r0 + CHUNK]
    tail = lax.dot_general(key * live, val, (((0,), (0,)), ((), ())), preferred_element_type=F32)
    return key, val, tail


def lanes(head, count=1):
    return pl.ds(pl.multiple_of(head * HEAD, HEAD), count * HEAD)


def run(copies):
    for copy in copies:
        copy.start()


def finish_all(copies):
    for copy in copies:
        copy.wait()


def late_kernel(
    here_ref, len_ref, k_hbm, v_hbm, w_ref,
    pk_hbm, val_hbm, st_ref, gate_ref, k0_ref, v0_ref, m0_ref, live0_ref,
    doc_s, m_s, live_s, ext_k, ext_v, kb, vb, pkb, valb, in_sem, out_sem, edge_sem,
    *, chips,
):
    rows = k_hbm.shape[0]
    chunks = rows // CHUNK
    pairs = kb.shape[0]
    tail_rows = pl.ds(CHUNK - GROUP, rows - CHUNK + GROUP)

    def head_of(p):
        return 2 * ((p + (1 - here_ref[0] % 2) * (pairs // 2)) % pairs)

    def fetch(p):
        cols = lanes(head_of(p), 2)
        return [
            pltpu.make_async_copy(k_hbm.at[tail_rows, cols], kb.at[p], in_sem.at[0, p]),
            pltpu.make_async_copy(v_hbm.at[tail_rows, cols], vb.at[p], in_sem.at[1, p]),
        ]

    def store(p):
        two = pl.ds(2 * p, 2)
        return [
            pltpu.make_async_copy(pkb.at[two], pk_hbm.at[two], out_sem.at[0, p]),
            pltpu.make_async_copy(valb.at[two], val_hbm.at[two], out_sem.at[1, p]),
        ]

    edges = [
        pltpu.make_async_copy(k_hbm.at[pl.ds(0, CHUNK)], k0_ref, edge_sem.at[0]),
        pltpu.make_async_copy(v_hbm.at[pl.ds(0, CHUNK)], v0_ref, edge_sem.at[1]),
    ]
    for p in range(pairs):
        run(fetch(p))
    run(edges)

    here = here_ref[0]
    core = here % 2
    offset = here * rows
    starts = starts_of(len_ref[...])
    fill_doc(offset, starts, doc_s, m_s)
    fill_live(doc_s, live_s)
    m0_ref[...] = m_s[:, :CHUNK]
    live0_ref[...] = live_s[:CHUNK]
    chip = offset - core * rows
    chip_mark = lax.broadcasted_iota(jnp.int32, (chips + 8, HEAD), 0)
    mark = lax.broadcasted_iota(jnp.int32, (16, HEAD), 0)
    ends, _ = docs_of(chip_mark * (2 * rows) - 1, starts)
    mine, _ = docs_of(chip + mark * rows - 1, starts)
    inner, _ = docs_of(offset + mark * CHUNK - 1, starts)
    keep_first = one_if(mine[1:2] == mine[0:1])
    keep_second = one_if(mine[2:3] == mine[1:2])
    second = jnp.full((1, HEAD), core, jnp.int32) == 1
    gate_ref[0:chips] = one_if(ends[1 : chips + 1] == ends[0:chips])
    one, zero = jnp.ones((1, HEAD), F32), jnp.zeros((1, HEAD), F32)
    rest = [
        jnp.where(second, one, keep_second),
        jnp.where(second, keep_second, one),
        jnp.where(second, keep_first, one),
        jnp.where(second, one, zero),
        jnp.where(second, one, keep_first),
        jnp.where(second, zero, one),
    ]
    for n, row in enumerate(rest):
        gate_ref[chips + n : chips + n + 1] = row
    for i in range(1, chunks):
        gate_ref[chips + 7 + i : chips + 8 + i] = one_if(inner[i : i + 1] == inner[0:1])
    for i in range(2, chunks + 1):
        gate_ref[chips + 9 + i : chips + 10 + i] = one_if(inner[i : i + 1] == inner[1:2])

    @pl.loop(0, pairs)
    def _(p):
        finish_all(fetch(p))
        for n in (0, 1):
            cols = slice(n * HEAD, (n + 1) * HEAD)
            ext_k[n, CHUNK - 8 :] = kb[p, :, cols].astype(F32)
            ext_v[n, CHUNK - 8 :] = vb[p, :, cols].astype(F32)
        head = head_of(p)
        taps = [(0.5 * w_ref[1, :, lanes(head + n)], w_ref[2, :, lanes(head + n)]) for n in (0, 1)]
        states = [jnp.zeros((HEAD, HEAD), F32)] * 2
        for i in range(1, chunks):
            r0 = i * CHUNK
            same = one_if(doc_s[8 + r0 - 1 : 8 + r0] == doc_s[8 + r0 + CHUNK - 1 : 8 + r0 + CHUNK])
            for n in (0, 1):
                key, val, tail = kv_chunk(ext_k.at[n], ext_v.at[n], *taps[n], m_s, live_s, r0)
                pkb[2 * p + n, r0 - CHUNK : r0] = key
                valb[2 * p + n, r0 - CHUNK : r0] = val
                states[n] = states[n] * same + tail
                st_ref[head + n, i - 1] = states[n]

        @pl.when(p < pairs // 2)
        def _():
            run(store(p))

    finish_all(edges)
    for p in range(pairs // 2):
        finish_all(store(p))


def first_kernel(
    here_ref, gate_ref, k_ref, v_ref, m_ref, live_ref, rim_ref, w_ref, late_ref,
    st_ref, tail_ref, ext_k, ext_v,
    *, mine, chips,
):
    heads = tail_ref.shape[0]
    here = here_ref[0]
    base = (here % 2 if mine else 1 - here % 2) * heads
    count = late_ref.shape[1] + 1

    @pl.loop(0, heads // 2)
    def _(p):
        for n in (0, 1):
            cols = lanes(base + 2 * p + n)
            ext_k[n, 0:8] = rim_ref[1, :, cols].astype(F32)
            ext_v[n, 0:8] = rim_ref[2, :, cols].astype(F32)
            ext_k[n, 8:] = k_ref[:, cols].astype(F32)
            ext_v[n, 8:] = v_ref[:, cols].astype(F32)
        for n in (0, 1):
            h = 2 * p + n
            cols = lanes(base + h)
            _, _, tail = kv_chunk(
                ext_k.at[n], ext_v.at[n], 0.5 * w_ref[1, :, cols], w_ref[2, :, cols], m_ref, live_ref, 0
            )
            st_ref[h, 0] = tail.astype(BF16)
            for i in range(1, count):
                state = late_ref[base + h, i - 1] + tail * gate_ref[chips + 10 + i : chips + 11 + i]
                if i < count - 1:
                    st_ref[h, i] = state.astype(BF16)
            tail_ref[h] = state.astype(BF16)


def attend_kernel(
    here_ref, len_ref, q_hbm, k_hbm, v_hbm, rim_ref, w_ref, *rest, mine,
):
    if mine:
        pq_ref, mix_ref, doc_s, m_s, use_s, ext, ext_k, ext_v, allow_s, qb, k0b, v0b, in_sem = rest
    else:
        (pk_hbm, val_hbm, pq_out, mix_out, doc_s, m_s, use_s, ext, ext_k, ext_v, allow_s,
         qb, k0b, v0b, in_sem, kb, vb, pq_ref, mix_ref, late_sem, out_sem) = rest
    pairs, rows, _ = pq_ref.shape
    chunks = rows // CHUNK
    here = here_ref[0]
    base = (here % 2 if mine else 1 - here % 2) * 2 * pairs
    made = pl.ds(0, k0b.shape[1])

    def fetch(p):
        cols, two = lanes(base + 2 * p, 2), pl.ds(2 * p, 2)
        copies = [
            pltpu.make_async_copy(q_hbm.at[:, cols], qb.at[p], in_sem.at[0, p]),
            pltpu.make_async_copy(k_hbm.at[made, cols], k0b.at[p], in_sem.at[1, p]),
            pltpu.make_async_copy(v_hbm.at[made, cols], v0b.at[p], in_sem.at[2, p]),
        ]
        if not mine:
            copies += [
                pltpu.make_async_copy(pk_hbm.at[two], kb.at[p], late_sem.at[0, p]),
                pltpu.make_async_copy(val_hbm.at[two], vb.at[p], late_sem.at[1, p]),
            ]
        return copies

    def store(p):
        return [
            pltpu.make_async_copy(pq_ref.at[p], pq_out.at[p], out_sem.at[0, p]),
            pltpu.make_async_copy(mix_ref.at[p], mix_out.at[p], out_sem.at[1, p]),
        ]

    for p in range(pairs):
        run(fetch(p))

    below = fill_doc(here * rows, starts_of(len_ref[...]), doc_s, m_s)
    across = lax.dot_general(
        jnp.ones((8, HEAD), BF16), below[8:], (((1,), (1,)), ((), ())), preferred_element_type=F32
    )
    causal = lax.broadcasted_iota(jnp.int32, (CHUNK, CHUNK), 1) <= lax.broadcasted_iota(
        jnp.int32, (CHUNK, CHUNK), 0
    )
    for i in range(chunks):
        r0 = i * CHUNK
        doc = doc_s[8 + r0 : 8 + r0 + CHUNK]
        same = wide(doc) == across[0:1, r0 : r0 + CHUNK]
        allow_s[i] = jnp.where(same & causal, 1.0, 0.0).astype(BF16)
        use_s[r0 : r0 + CHUNK] = one_if(doc == doc_s[8 + r0 - 1 : 8 + r0]).astype(BF16)

    @pl.loop(0, pairs)
    def _(p):
        finish_all(fetch(p))
        taps = []
        for n in (0, 1):
            cols, head = slice(n * HEAD, (n + 1) * HEAD), lanes(base + 2 * p + n)
            for which, buffer, rows in ((0, ext, qb), (1, ext_k, k0b), (2, ext_v, v0b)):
                buffer[n, 0:8] = rim_ref[which, :, head].astype(F32)
                buffer[n, 8:] = rows[p, :, cols].astype(F32)
            taps.append((0.5 * w_ref[0, :, head], 0.5 * w_ref[1, :, head], w_ref[2, :, head]))

        def make(i, n):
            r0 = i * CHUNK
            rows = slice(r0, r0 + CHUNK)
            query = silu_of_half(conv(ext.at[n], taps[n][0], m_s, r0)).astype(BF16)
            pq_ref[p, rows, n * HEAD : (n + 1) * HEAD] = query * use_s[rows]
            if mine or i == 0:
                key = silu_of_half(conv(ext_k.at[n], taps[n][1], m_s, r0)).astype(BF16)
                val = conv(ext_v.at[n], taps[n][2], m_s, r0).astype(BF16)
            else:
                key, val = kb[p, n, r0 - CHUNK : r0], vb[p, n, r0 - CHUNK : r0]
            return query, key, val

        def mixed(i, n, query, key, val):
            scores = lax.dot_general(query, key, (((1,), (1,)), ((), ())), preferred_element_type=F32)
            weights = scores.astype(BF16) * allow_s[i]
            mix = jnp.dot(weights, val, preferred_element_type=F32)
            mix_ref[p, i * CHUNK : (i + 1) * CHUNK, n * HEAD : (n + 1) * HEAD] = mix.astype(BF16)

        ahead = None
        for i in range(chunks):
            for n in (0, 1):
                made_now = make(i, n)
                if ahead is not None:
                    mixed(*ahead)
                ahead = (i, n) + made_now
        mixed(*ahead)
        if not mine:
            run(store(p))

    if not mine:
        for p in range(pairs):
            finish_all(store(p))


def both(first, second):
    none = jnp.zeros_like(first)
    return jnp.concatenate(
        [jnp.concatenate([first, none], axis=1), jnp.concatenate([none, second], axis=1)], axis=0
    )


def finish_kernel(here_ref, gate_ref, pq_ref, mix_ref, st_ref, carried_ref, gain_ref, *rest, mine, chips):
    if mine:
        pqx_hbm, mixx_hbm, out_hbm, pqx_ref, mixx_ref, outb, out_sem, next_sem = rest
        onward = [
            pltpu.make_async_copy(pqx_hbm, pqx_ref, next_sem.at[0]),
            pltpu.make_async_copy(mixx_hbm, mixx_ref, next_sem.at[1]),
        ]
    else:
        _, out_hbm, outb, out_sem = rest
        onward = []
    pairs, rows, _ = pq_ref.shape
    chunks = rows // CHUNK
    base = (here_ref[0] % 2 if mine else 1 - here_ref[0] % 2) * 2 * pairs
    mean = both(jnp.full((HEAD, HEAD), 1.0 / HEAD, BF16), jnp.full((HEAD, HEAD), 1.0 / HEAD, BF16))
    run(onward)

    def store(p, i):
        rows = pl.ds(i * CHUNK, CHUNK)
        return pltpu.make_async_copy(
            outb.at[p, rows], out_hbm.at[rows, lanes(base + 2 * p, 2)], out_sem.at[p, i]
        )

    @pl.loop(0, pairs)
    def _(p):
        gain = gain_ref[:, lanes(base + 2 * p, 2)]

        def entering(h, i):
            if not i:
                return carried_ref[h]
            kept = carried_ref[h].astype(F32) * gate_ref[chips + 7 + i : chips + 8 + i]
            return (st_ref[h, i - 1].astype(F32) + kept).astype(BF16)

        def blend(at, state):
            held = jnp.dot(pq_ref[p, at : at + BLOCK], state, preferred_element_type=F32)
            return mix_ref[p, at : at + BLOCK].astype(F32) + held

        def norm(at, mixture):
            square = jnp.dot((mixture * mixture).astype(BF16), mean, preferred_element_type=F32)
            scale = lax.rsqrt(square + 1e-06) * gain
            outb[p, at : at + BLOCK] = (mixture * scale).astype(BF16)
            if (at + BLOCK) % CHUNK == 0:
                store(p, at // CHUNK).start()

        ahead = None
        for i in range(chunks):
            state = both(entering(2 * p, i), entering(2 * p + 1, i))
            for at in range(i * CHUNK, (i + 1) * CHUNK, BLOCK):
                mixture = blend(at, state)
                if ahead is not None:
                    norm(*ahead)
                ahead = (at, mixture)
        norm(*ahead)

    finish_all(onward)
    for p in range(pairs):
        for i in range(chunks):
            store(p, i).wait()


def rim_kernel(q_ref, k_ref, v_ref, out_ref):
    out_ref[0] = q_ref[...]
    out_ref[1] = k_ref[...]
    out_ref[2] = v_ref[...]


def join_kernel(gate_ref, own_ref, got_ref, out_ref, *, chips):
    own, got = gate_ref[chips : chips + 1], gate_ref[chips + 1 : chips + 2]
    out_ref[...] = (own_ref[...].astype(F32) * own + got_ref[...].astype(F32) * got).astype(BF16)


def enter_kernel(gate_ref, spread_ref, out_ref, *, counted):
    running = jnp.zeros(spread_ref.shape[1:], F32)
    for chip in range(spread_ref.shape[0]):
        n = counted.index(chip)
        out_ref[n] = running.astype(BF16)
        running = running * gate_ref[chip : chip + 1] + spread_ref[n].astype(F32)


def carry_kernel(gate_ref, entered_ref, own_ref, got_ref, mine_ref, other_ref, *, chips):
    gate = [gate_ref[chips + 2 + n : chips + 3 + n] for n in range(4)]
    entered = entered_ref[...].astype(F32)
    mine_ref[...] = (entered * gate[0] + got_ref[...].astype(F32) * gate[1]).astype(BF16)
    other_ref[...] = (entered * gate[2] + own_ref[...].astype(F32) * gate[3]).astype(BF16)


def in_hbm(x):
    return pltpu.with_memory_space_constraint(x, pltpu.HBM)


def params(mib):
    return pltpu.CompilerParams(vmem_limit_bytes=mib * 1024 * 1024)


def small(kernel, outs, *args):
    return pl.pallas_call(
        kernel, out_shape=outs, compiler_params=pltpu.CompilerParams(vmem_limit_bytes=4 * 1024 * 1024)
    )(*args)


def shaped(*shape, dtype=BF16):
    return jax.ShapeDtypeStruct(shape, dtype)


def per_device(query_rows, key_rows, value_rows, lengths, conv_weight, out_gain):
    query_rows, key_rows, value_rows = (in_hbm(x) for x in (query_rows, key_rows, value_rows))
    rows, channels = query_rows.shape
    heads = channels // HEAD
    half = heads // 2
    chunks = rows // CHUNK
    ctx_count = lax.axis_size(CTX)
    chips = ctx_count // 2
    z_chips = chips // X_CHIPS
    counted = [
        (FIRST_X + x) % X_CHIPS * z_chips + (FIRST_Z + z) % z_chips for x in range(X_CHIPS) for z in range(z_chips)
    ]
    groups = [[2 * chip + core for chip in counted] for core in (0, 1)]
    here = lax.axis_index(CTX).astype(jnp.int32).reshape(1)
    swap = [(i, i ^ 1) for i in range(ctx_count)]

    smem = pl.BlockSpec(memory_space=pltpu.SMEM)
    last_rows = pl.BlockSpec((8, channels), lambda i: (rows // 8 - 1, 0))
    rims = pl.pallas_call(
        rim_kernel,
        grid=(1,),
        in_specs=[last_rows] * 3,
        out_specs=pl.BlockSpec((3, 8, channels), lambda i: (0, 0, 0)),
        out_shape=shaped(3, 8, channels),
        compiler_params=params(4),
        name="rim",
    )(query_rows, key_rows, value_rows)
    rims = lax.ppermute(rims, CTX, [(i, (i + 1) % ctx_count) for i in range(ctx_count)])

    vmem = pl.BlockSpec(memory_space=pltpu.VMEM)
    hbm = pl.BlockSpec(memory_space=pl.ANY)
    lengths = lengths.reshape(1, -1)
    gains = out_gain.reshape(1, -1)
    gate_rows = chips + 16
    pairs, half_pairs = heads // 2, half // 2
    later = rows - CHUNK
    dma = lambda *shape: pltpu.SemaphoreType.DMA(shape)

    def masks(count):
        return [
            pltpu.VMEM((count + 8, HEAD), F32),
            pltpu.VMEM((3, count, HEAD), F32),
            pltpu.VMEM((count, HEAD), BF16),
        ]

    pk_late, val_late, st_late, gates, key_head, value_head, inside, live = pl.pallas_call(
        lambda *refs: late_kernel(*refs, chips=chips),
        in_specs=[smem, vmem, hbm, hbm, vmem],
        out_specs=[hbm, hbm] + [vmem] * 6,
        out_shape=[
            pltpu.HBM((half, later, HEAD), BF16),
            pltpu.HBM((half, later, HEAD), BF16),
            shaped(heads, chunks - 1, HEAD, HEAD, dtype=F32),
            shaped(gate_rows, HEAD, dtype=F32),
            shaped(CHUNK, channels),
            shaped(CHUNK, channels),
            shaped(3, CHUNK, HEAD, dtype=F32),
            shaped(CHUNK, HEAD),
        ],
        scratch_shapes=masks(rows)
        + [pltpu.VMEM((2, rows + 8, HEAD), F32)] * 2
        + [pltpu.VMEM((pairs, later + GROUP, 2 * HEAD), BF16)] * 2
        + [pltpu.VMEM((heads, later, HEAD), BF16)] * 2
        + [dma(2, pairs), dma(2, half_pairs), dma(2)],
        compiler_params=params(20),
        name="late",
    )(here, lengths, key_rows, value_rows, conv_weight)
    pk_late, val_late = in_hbm(pk_late), in_hbm(val_late)

    def first(mine):
        return pl.pallas_call(
            lambda *refs: first_kernel(*refs, mine=mine, chips=chips),
            in_specs=[smem] + [vmem] * 8,
            out_specs=[vmem] * 2,
            out_shape=[
                shaped(half, chunks - 1, HEAD, HEAD),
                shaped(half, HEAD, HEAD),
            ],
            scratch_shapes=[pltpu.VMEM((2, CHUNK + 8, HEAD), F32)] * 2,
            compiler_params=params(8),
            name="first",
        )(here, gates, key_head, value_head, inside, live, rims, conv_weight, st_late)

    inner_other, other = first(False)
    got = lax.ppermute(other, CTX, swap)
    inner_own, own = first(True)

    state = (half, HEAD, HEAD)
    chip_tail = small(lambda *r: join_kernel(*r, chips=chips), shaped(*state), gates, own, got)
    spread = lax.all_to_all(chip_tail.reshape(chips, -1, HEAD), CTX, 0, 0, axis_index_groups=groups, tiled=True)

    def attend(mine, *ready):
        shape = (half_pairs, rows, 2 * HEAD)
        made = rows if mine else CHUNK
        return pl.pallas_call(
            lambda *refs: attend_kernel(*refs, mine=mine),
            in_specs=[smem, vmem, hbm, hbm, hbm, vmem, vmem] + [hbm] * len(ready),
            out_specs=[vmem if mine else hbm] * 2,
            out_shape=[shaped(*shape) if mine else pltpu.HBM(shape, BF16)] * 2,
            scratch_shapes=masks(rows)
            + [pltpu.VMEM((2, rows + 8, HEAD), F32)]
            + [pltpu.VMEM((2, made + 8, HEAD), F32)] * 2
            + [pltpu.VMEM((chunks, CHUNK, CHUNK), BF16), pltpu.VMEM(shape, BF16)]
            + [pltpu.VMEM((half_pairs, made, 2 * HEAD), BF16)] * 2
            + [dma(3, half_pairs)]
            + (
                []
                if mine
                else [pltpu.VMEM((half_pairs, 2, later, HEAD), BF16)] * 2
                + [pltpu.VMEM(shape, BF16)] * 2
                + [dma(2, half_pairs)] * 2
            ),
            compiler_params=params(24),
            name="attend",
        )(here, lengths, query_rows, key_rows, value_rows, rims, conv_weight, *ready)

    phi_other, mix_other = (in_hbm(x) for x in attend(False, pk_late, val_late))
    phi_own, mix_own = attend(True)

    entering = small(lambda *r: enter_kernel(*r, counted=counted), shaped(*spread.shape), gates, spread)
    entered = lax.all_to_all(entering, CTX, 0, 0, axis_index_groups=groups, tiled=True).reshape(state)
    carried_own, carried_other = small(
        lambda *r: carry_kernel(*r, chips=chips), [shaped(*state)] * 2, gates, entered, own, got
    )
    carried_far = lax.ppermute(carried_other, CTX, swap)

    def finish(mine, phi, mix, inner, carried, *others):
        shape = (half_pairs, rows, 2 * HEAD)
        ahead = [shaped(*shape)] * 2 if mine else []
        args = (here, gates, phi, mix, inner, carried, gains, *others)
        return pl.pallas_call(
            lambda *refs: finish_kernel(*refs, mine=mine, chips=chips),
            in_specs=[smem] + [vmem] * 6 + [hbm] * len(others),
            out_specs=[hbm] + [vmem] * len(ahead),
            out_shape=[pltpu.HBM((rows, channels), BF16)] + ahead,
            scratch_shapes=[pltpu.VMEM((half_pairs, rows, 2 * HEAD), BF16), dma(half_pairs, chunks)]
            + ([dma(2)] if mine else []),
            input_output_aliases={} if mine else {len(args) - 1: 0},
            compiler_params=params(12),
            name="finish",
        )(*args)

    done, phi_other, mix_other = finish(
        True, phi_own, mix_own, inner_own, carried_own, phi_other, mix_other
    )
    return finish(False, phi_other, mix_other, inner_other, carried_far, done)[0]


def solution(mesh):
    return jax.shard_map(
        per_device,
        mesh=mesh,
        in_specs=(P(DP_CTX, None), P(DP_CTX, None), P(DP_CTX, None), P("dp"), P(), P()),
        out_specs=P(DP_CTX, None),
        check_vma=False,
    )
```
